32 devices in a mesh: azim: 8 (over z, y), dom: 4 (over x, core).
Axes of the slice: x: 2, y: 2, z: 4, core: 2. Of those that a mesh axis runs over, the one named last changes fastest.
Arguments:
- search_basis: float32 [16, 2, 16, 64, 512], P(None, None, 'azim', 'dom'), may hold values from -4 to 4
- coefficients: float32 [2, 16], replicated, may hold values from -4 to 4
- target_shift: float32 [2], replicated, may hold values from 1.5 to 2.5
- stiffness_diag: float32 [16, 64, 512], P('azim', 'dom'), may hold values from 0.25 to 2
- flame_mats: bfloat16 [256, 2, 512, 512], P(('azim', 'dom')), may hold values from -0.5 to 0.5
- flame_count: int32 [32], P(('azim', 'dom')), may hold values from 0 to 8, as said below
- flame_line: int32 [256], P(('azim', 'dom')), may hold values from 16 to 31
- flame_burner: int32 [256], P(('azim', 'dom')), may hold values from 0 to 1
- reference_part: int32 [16], P('azim'), may hold values from 0 to 3
- reference_line: int32 [16], P('azim'), may hold values from 0 to 15
Outputs:
- new_vector: float32 [2, 16, 64, 512], P(None, 'azim', 'dom')
- ritz_value: float32 [2], replicated
The draws below stay inside these ranges and needn't reach their ends.
Inputs may be any that keep to these rules, and one draw needn't show every extreme that they name: `flame_count`: in each sector exactly two devices hold 8 live flame slots; each other device holds none or one. Live slots come first on a device. `flame_line`: flame lines lie at local indices 16 or more, reference lines below 16, so the two never coincide.
All inputs are finite; a program needn't handle non-finite values.
Results may differ from the reference program's by a relative error of at most 0.0012.
Values may be sent and summed in bfloat16 or wider, within the bound.
No kernel may reach another device: no remote copies, remote signals or barrier semaphores. Data moves between devices by JAX's collectives and lax.ppermute only.
A program may use at most 64 MiB of HBM per device.

```python
import jax
import jax.numpy as jnp
from jax import lax

SECTOR_ROWS = 2
PART_ROWS = 16
LINE_DOFS = 512
SEARCH_VECTORS = 16
INNER_STEPS = 3
SLOTS_DEV = 8
BURNERS_SECTOR = 2
AZIM_CELLS = 16
RADIAL_CELLS = 64
BURNERS = 16
SLOTS = 256
N_AZIM = 8
N_DOM = 4


def draw_flame_count(key, part):
    sectors = N_AZIM
    sector_keys = jax.random.split(jax.random.fold_in(key, 11), sectors)
    ranks = jax.vmap(lambda one_key: jax.random.permutation(one_key, N_DOM))(sector_keys)
    light = jax.random.randint(jax.random.fold_in(key, 12), (sectors, N_DOM), 0, 2)
    counts = jnp.where(ranks < 2, SLOTS_DEV, light)
    return counts.reshape(N_AZIM * N_DOM).astype(jnp.int32)


def draw_search_basis(key, part):
    frequency = jax.random.permutation(jax.random.fold_in(key, 21), LINE_DOFS)[:SEARCH_VECTORS].astype(jnp.int32)
    position = jnp.arange(LINE_DOFS, dtype=jnp.int32)
    phase_index = frequency[:, None] * (2 * position[None, :] + 1) % (4 * LINE_DOFS)
    angle = jnp.pi / (2.0 * LINE_DOFS) * phase_index.astype(jnp.float32)
    amplitude = jnp.where(frequency == 0, 1.0, jnp.sqrt(2.0)).astype(jnp.float32)
    modes = amplitude[:, None] * jnp.cos(angle)
    line_shape = (SEARCH_VECTORS, 2, AZIM_CELLS, RADIAL_CELLS, 1)
    factors = jnp.sqrt(0.5) * jnp.clip(jax.random.normal(jax.random.fold_in(key, 23), line_shape, jnp.float32), -4.0, 4.0)
    values = factors * modes[:, None, None, None, :]
    return jnp.clip(values, -4.0, 4.0).astype(jnp.float32)


def place_ends(array, key, least, largest):
    extent = array.shape
    spot = [jax.random.randint(jax.random.fold_in(key, axis), (), 0, extent[axis]) for axis in range(len(extent))]
    array = array.at[tuple(spot)].set(least)
    longest = extent.index(max(extent))
    spot[longest] = (spot[longest] + 1) % extent[longest]
    return array.at[tuple(spot)].set(largest)


def shard_levels(stream_key, dims, shards, least, high):
    loudness = 1.0
    for axis_at, parts in shards:
        steps = jax.random.uniform(jax.random.fold_in(jax.random.fold_in(stream_key, 6), axis_at), (parts,), jnp.float32, least / len(shards), high / len(shards))
        loudness = loudness * jnp.repeat(jnp.exp(steps), dims[axis_at] // parts).reshape((-1,) + (1,) * (len(dims) - 1 - axis_at))
    return loudness


def normal_values(key, dims, width, reach, cuts=(), kind=jnp.bfloat16):
    entries = jax.random.normal(key, dims, jnp.float32) * width
    if len(cuts) > 0:
        entries = shard_levels(key, dims, cuts, -0.22, 0.18) * entries
    return jnp.clip(entries, min=-reach, max=reach).astype(kind)


def setup_inputs(seed: int = 0) -> dict:
    streams_of = jax.random.split(jax.random.key(seed), 11)
    return {
        "search_basis": draw_search_basis(jax.random.fold_in(streams_of[10], 71), 0),
        "coefficients": normal_values(streams_of[1], (2, SEARCH_VECTORS), 1.0, 4.0, (), jnp.float32),
        "target_shift": jnp.clip(jax.random.uniform(streams_of[2], (2,), jnp.float32, 1.5, 2.5), 1.5, 2.5),
        "stiffness_diag": jnp.clip(0.25 + 1.75 * jax.random.uniform(streams_of[3], (AZIM_CELLS, RADIAL_CELLS, LINE_DOFS), jnp.float32) ** shard_levels(streams_of[3], (AZIM_CELLS, RADIAL_CELLS, LINE_DOFS), ((0, 8), (1, 4)), -0.2, 0.2), 0.25, 2.0),
        "flame_mats": normal_values(streams_of[4], (SLOTS, 2, LINE_DOFS, LINE_DOFS), (LINE_DOFS // 4) ** -0.5, 0.5, ((0, 32),)),
        "flame_count": draw_flame_count(jax.random.fold_in(streams_of[10], 71), 0),
        "flame_line": place_ends(jax.random.randint(streams_of[6], (SLOTS,), PART_ROWS, SECTOR_ROWS * PART_ROWS), jax.random.fold_in(streams_of[6], 1), PART_ROWS, (SECTOR_ROWS * PART_ROWS) - 1).astype(jnp.int32),
        "flame_burner": place_ends(jax.random.randint(streams_of[7], (SLOTS,), 0, BURNERS_SECTOR), jax.random.fold_in(streams_of[7], 1), 0, BURNERS_SECTOR - 1).astype(jnp.int32),
        "reference_part": place_ends(jax.random.randint(streams_of[8], (BURNERS,), 0, N_DOM), jax.random.fold_in(streams_of[8], 1), 0, N_DOM - 1).astype(jnp.int32),
        "reference_line": place_ends(jax.random.randint(streams_of[9], (BURNERS,), 0, PART_ROWS), jax.random.fold_in(streams_of[9], 1), 0, PART_ROWS - 1).astype(jnp.int32),
    }


EPSILON = 1e-06
PRECISION_HIGH = lax.Precision.HIGHEST

def inner_many(stacked, vector, dof_total):
    flat_many = stacked.reshape(stacked.shape[0], 2, -1)
    flat_one = vector.reshape(2, -1)
    cross = jnp.einsum('kcn,dn->kcd', flat_many, flat_one, precision=PRECISION_HIGH)
    return ((cross[:, 0, 0] + cross[:, 1, 1]) / dof_total, (cross[:, 0, 1] - cross[:, 1, 0]) / dof_total)

def combine(coef_re, coef_im, stacked):
    real_part = jnp.einsum('k,k...->...', coef_re, stacked[:, 0], precision=PRECISION_HIGH) - jnp.einsum('k,k...->...', coef_im, stacked[:, 1], precision=PRECISION_HIGH)
    imag_part = jnp.einsum('k,k...->...', coef_re, stacked[:, 1], precision=PRECISION_HIGH) + jnp.einsum('k,k...->...', coef_im, stacked[:, 0], precision=PRECISION_HIGH)
    return jnp.stack([real_part, imag_part])

def scale_field(scale_re, scale_im, vector):
    return jnp.stack([scale_re * vector[0] - scale_im * vector[1], scale_re * vector[1] + scale_im * vector[0]])

def flame_product(matrix, source):
    size_line = matrix.shape[1]
    product = jnp.dot(matrix.reshape(2 * size_line, size_line).astype(jnp.float32), source.T.astype(jnp.float32), preferred_element_type=jnp.float32)
    return jnp.stack([product[:size_line, 0] - product[size_line:, 1], product[:size_line, 1] + product[size_line:, 0]])

def least_squares(hess_re, hess_im, beta):
    columns = hess_re.shape[1]
    upper = jnp.concatenate([hess_re, -hess_im], axis=1)
    lower = jnp.concatenate([hess_im, hess_re], axis=1)
    system = jnp.concatenate([upper, lower], axis=0)
    wanted = jnp.zeros((system.shape[0],), system.dtype).at[0].set(beta)
    normal = jnp.dot(system.T, system, precision=PRECISION_HIGH)
    moment = jnp.dot(system.T, wanted, precision=PRECISION_HIGH)
    factor = jnp.linalg.cholesky(normal)
    middle = lax.linalg.triangular_solve(factor, moment[:, None], left_side=True, lower=True)
    solved = lax.linalg.triangular_solve(factor, middle, left_side=True, lower=True, transpose_a=True)
    return (solved[:columns, 0], solved[columns:, 0])

def stiffness(vector, stiffness_diag):
    beside_all = jnp.roll(vector, -1, axis=1) + jnp.roll(vector, 1, axis=1)
    padded = jnp.pad(vector, ((0, 0), (0, 0), (1, 1), (1, 1)))
    radial = padded[:, :, 2:, 1:-1] + padded[:, :, :-2, 1:-1]
    along = padded[:, :, 1:-1, 2:] + padded[:, :, 1:-1, :-2]
    return (6.0 + stiffness_diag) * vector - (beside_all + radial + along)

def flame_term(vector, flame_mats, flame_count, flame_line, flame_burner, reference_part, reference_line):
    slot_ids = jnp.arange(SLOTS, dtype=jnp.int32)
    device = slot_ids // SLOTS_DEV
    sector = device // N_DOM
    mesh_part = device % N_DOM
    live = slot_ids % SLOTS_DEV < flame_count[device]
    burner_ids = jnp.arange(BURNERS, dtype=jnp.int32)
    burner_sector = burner_ids // BURNERS_SECTOR
    ref_azim = burner_sector * SECTOR_ROWS + reference_line // PART_ROWS
    ref_radial = reference_part * PART_ROWS + reference_line % PART_ROWS
    burner_rows = vector[:, ref_azim, ref_radial, :].astype(jnp.bfloat16)
    global_burner = sector * BURNERS_SECTOR + flame_burner

    def one_slot(slot):
        product = flame_product(flame_mats[slot], burner_rows[:, global_burner[slot], :])
        return jnp.where(live[slot], product, jnp.zeros_like(product))
    products = lax.map(one_slot, slot_ids)
    target_azim = sector * SECTOR_ROWS + flame_line // PART_ROWS
    target_radial = mesh_part * PART_ROWS + flame_line % PART_ROWS
    return jnp.zeros_like(vector).at[:, target_azim, target_radial, :].add(jnp.transpose(products, (1, 0, 2)))

def reference(search_basis, coefficients, target_shift, stiffness_diag, flame_mats, flame_count, flame_line, flame_burner, reference_part, reference_line):
    dof_total = float(AZIM_CELLS * RADIAL_CELLS * LINE_DOFS)

    def operate(vector):
        stiffness_part = stiffness(vector, stiffness_diag)
        flame_part = flame_term(vector, flame_mats, flame_count, flame_line, flame_burner, reference_part, reference_line)
        return stiffness_part - scale_field(target_shift[0], target_shift[1], vector) + flame_part

    def norm_of(vector):
        squared = inner_many(vector[None], vector, dof_total)[0][0]
        return jnp.sqrt(squared + EPSILON)
    start = combine(coefficients[0], coefficients[1], search_basis)
    ritz_vector = start / norm_of(start)
    image = operate(ritz_vector)
    image_sq = inner_many(image[None], image, dof_total)[0][0]
    cross_re, cross_im = inner_many(image[None], ritz_vector, dof_total)
    denominator = cross_re[0] * cross_re[0] + cross_im[0] * cross_im[0]
    theta_re = image_sq * cross_re[0] / denominator
    theta_im = -image_sq * cross_im[0] / denominator
    residual = image - scale_field(theta_re, theta_im, ritz_vector)
    along_re, along_im = inner_many(ritz_vector[None], residual, dof_total)
    right_side = -(residual - scale_field(along_re[0], along_im[0], ritz_vector))
    beta = norm_of(right_side)
    krylov = [right_side / beta]
    hess_re = jnp.zeros((INNER_STEPS + 1, INNER_STEPS), jnp.float32)
    hess_im = jnp.zeros((INNER_STEPS + 1, INNER_STEPS), jnp.float32)
    for column in range(INNER_STEPS):
        current = krylov[-1]
        candidate = operate(current) - scale_field(theta_re, theta_im, current)
        proj_re, proj_im = inner_many(ritz_vector[None], candidate, dof_total)
        candidate = candidate - scale_field(proj_re[0], proj_im[0], ritz_vector)
        stacked = jnp.stack(krylov)
        dots_re, dots_im = inner_many(stacked, candidate, dof_total)
        candidate = candidate - combine(dots_re, dots_im, stacked)
        length = norm_of(candidate)
        hess_re = hess_re.at[:column + 1, column].set(dots_re)
        hess_im = hess_im.at[:column + 1, column].set(dots_im)
        hess_re = hess_re.at[column + 1, column].set(length)
        if column + 1 < INNER_STEPS:
            krylov.append(candidate / length)
    solve_re, solve_im = least_squares(hess_re, hess_im, beta)
    update = combine(solve_re, solve_im, jnp.stack(krylov))
    for repeat in range(2):
        basis_re, basis_im = inner_many(search_basis, update, dof_total)
        update = update - combine(basis_re, basis_im, search_basis)
    new_vector = update / norm_of(update)
    return (new_vector, jnp.stack([theta_re, theta_im]))
```

```python
import functools

import jax
import jax.numpy as jnp
from jax import lax
from jax.experimental import pallas as pl
from jax.experimental.pallas import tpu as pltpu
from jax.sharding import PartitionSpec as P

INNER_STEPS = 3
EPSILON = 1e-06
CENTRE = 7.125
HIGHEST = lax.Precision.HIGHEST
VMEM = pltpu.VMEM
SMEM = pltpu.SMEM


def vmem(count):
    return [pl.BlockSpec(memory_space=VMEM) for _ in range(count)]


def smem(count):
    return [pl.BlockSpec(memory_space=SMEM) for _ in range(count)]


def call(kernel, outs, specs, args, scratch=(), cost=None, limit=16 << 20):
    return pl.pallas_call(
        kernel,
        out_shape=outs,
        in_specs=specs,
        out_specs=jax.tree.map(lambda _: pl.BlockSpec(memory_space=VMEM), outs),
        scratch_shapes=list(scratch),
        compiler_params=pltpu.CompilerParams(vmem_limit_bytes=limit),
        cost_estimate=cost,
    )(*args)


def write_edges(rows, depth, field, ref_part, ref_line, azim_x, azim_y, dom_x, dom_y):
    odd_a = lax.axis_index("azim") % 2
    part = lax.axis_index("dom")
    odd_d = part % 2
    last = (rows - 1) * depth
    x_start = pl.multiple_of((1 - odd_a) * last, depth)
    y_start = pl.multiple_of(odd_a * last, depth)
    for c in range(2):
        azim_x[c] = field[c, pl.ds(x_start, depth), :]
        azim_y[c] = field[c, pl.ds(y_start, depth), :]
        for a in range(rows):
            x_row = a * depth + (1 - odd_d) * (depth - 1)
            y_row = a * depth + odd_d * (depth - 1)
            at = c * rows + a
            dom_x[at : at + 1, :] = field[c, pl.ds(x_row, 1), :]
            dom_y[at : at + 1, :] = field[c, pl.ds(y_row, 1), :]
    base = 2 * rows
    for b in range(ref_part.shape[0]):
        mine = ref_part[b] == part
        for c in range(2):
            at = base + 2 * b + c
            line = field[c, pl.ds(ref_line[b], 1), :]
            dom_x[at : at + 1, :] = jnp.where(mine, line, 0.0)
            dom_y[at : at + 1, :] = jnp.zeros_like(line)


def start_kernel(rows, depth, coef, ref_part, ref_line, basis, field, azim_x, azim_y, dom_x, dom_y):
    count = basis.shape[0]
    for a in range(rows):
        span = slice(a * depth, (a + 1) * depth)
        real = jnp.zeros((depth, basis.shape[3]), jnp.float32)
        imag = real
        for i in range(count):
            re, im = basis[i, 0, span, :], basis[i, 1, span, :]
            real = real + (coef[0, i] * re - coef[1, i] * im)
            imag = imag + (coef[0, i] * im + coef[1, i] * re)
        field[0, span, :] = real
        field[1, span, :] = imag
    write_edges(rows, depth, field, ref_part, ref_line, azim_x, azim_y, dom_x, dom_y)


def flame_kernel(base, k, live, lines, burners, mats, sums, basis, *refs):
    powers, (out, dots_out, source, held) = refs[: k + 1], refs[-4:]
    dots_in = refs[k + 1] if k else None
    add_dots(k, basis, powers[:-1], powers[-1], dots_in, dots_out, held)
    width = sums.shape[1]
    count = (sums.shape[0] - base) // 2
    for b in range(count):
        for c in range(2):
            row = sums[base + 2 * b + c : base + 2 * b + c + 1, :]
            high = row.astype(jnp.bfloat16)
            low = (row - high.astype(jnp.float32)).astype(jnp.bfloat16)
            source[b, 2 * c : 2 * c + 1, :] = high
            source[b, 2 * c + 1 : 2 * c + 2, :] = low
    out[...] = jnp.zeros_like(out)

    def slot(s, carry):
        product = lax.dot_general(
            source[burners[s]],
            mats[s],
            (((1,), (1,)), ((), ())),
            preferred_element_type=jnp.float32,
        )
        by_re = product[0:1] + product[1:2]
        by_im = product[2:3] + product[3:4]
        at = pl.ds(lines[s], 1)
        out[0, at, :] += by_re[:, :width] - by_im[:, width:]
        out[1, at, :] += by_im[:, :width] + by_re[:, width:]
        return carry

    lax.fori_loop(0, live[0], slot, 0)


def step_kernel(
    rows, depth, ref_part, ref_line, old, flame, diag, from_ax, from_ay, from_dx, from_dy,
    field, azim_x, azim_y, dom_x, dom_y,
):
    width = old.shape[2]
    odd_a = lax.axis_index("azim") % 2 == 1
    part = lax.axis_index("dom")
    odd_d = part % 2 == 1
    row_at = lax.broadcasted_iota(jnp.int32, (depth, width), 0)
    lane_at = lax.broadcasted_iota(jnp.int32, (depth, width), 1)
    for c in range(2):
        before = jnp.where(odd_a, from_ax[c], from_ay[c])
        after = jnp.where(odd_a, from_ay[c], from_ax[c])
        planes = [old[c, a * depth : (a + 1) * depth, :] for a in range(rows)]
        around = [before, *planes, after]
        for a in range(rows):
            here = planes[a]
            at = c * rows + a
            one, two = from_dx[at : at + 1, :], from_dy[at : at + 1, :]
            inner = jnp.where(part == 0, 0.0, jnp.where(odd_d, one, two))
            outer = jnp.where(part == lax.axis_size("dom") - 1, 0.0, jnp.where(odd_d, two, one))
            down = jnp.where(row_at == 0, inner, pltpu.roll(here, 1, 0))
            up = jnp.where(row_at == depth - 1, outer, pltpu.roll(here, depth - 1, 0))
            left = jnp.where(lane_at == 0, 0.0, pltpu.roll(here, 1, 1))
            right = jnp.where(lane_at == width - 1, 0.0, pltpu.roll(here, width - 1, 1))
            beside = (around[a] + around[a + 2]) + (down + up) + (left + right)
            span = slice(a * depth, (a + 1) * depth)
            factor = diag[span, :] + (6.0 - CENTRE)
            field[c, span, :] = factor * here - beside + flame[c, span, :]
    if azim_x is not None:
        write_edges(rows, depth, field, ref_part, ref_line, azim_x, azim_y, dom_x, dom_y)


def last_kernel(rows, depth, *refs):
    first, powers, (dots_in, dots_out, field, held) = refs[:7], refs[7:-4], refs[-4:]
    step_kernel(rows, depth, None, None, *first, field, None, None, None, None)
    add_dots(len(powers), None, powers, field, dots_in, dots_out, held)


def folded(x):
    tall = total_of(x[i : i + 8] for i in range(0, x.shape[0], 8))
    tile = total_of(tall[:, j : j + 128] for j in range(0, x.shape[1], 128))
    return jnp.sum(tile, axis=0, keepdims=True)


def total_of(terms):
    terms = list(terms)
    while len(terms) > 1:
        terms = [
            terms[i] + terms[i + 1] if i + 1 < len(terms) else terms[i]
            for i in range(0, len(terms), 2)
        ]
    return terms[0]


def add_dots(k, basis, powers, current, dots_in, dots_out, held):
    held[...] = jnp.zeros_like(held)
    re, im = current[0], current[1]
    count = 0
    if basis is not None:
        count = basis.shape[0]

        def one(i, carry):
            left_re, left_im = basis[i, 0], basis[i, 1]
            held[pl.ds(i, 1), :] = folded(left_re * re + left_im * im)
            held[pl.ds(count + i, 1), :] = folded(left_re * im - left_im * re)
            return carry

        lax.fori_loop(0, count, one, 0)
    first = held.shape[0] - 16
    for j, power in enumerate([*powers, current]):
        left_re, left_im = power[0], power[1]
        held[first + j : first + j + 1, :] = folded(left_re * re + left_im * im)
        held[first + 8 + j : first + 9 + j, :] = folded(left_re * im - left_im * re)
    row = lax.dot_general(
        jnp.ones((8, 128), jnp.float32), held[...], (((1,), (1,)), ((), ())),
        precision=HIGHEST, preferred_element_type=jnp.float32,
    )
    at = lax.broadcasted_iota(jnp.int32, row.shape, 0)
    wide = row.shape[1]
    dots_out[...] = jnp.zeros_like(dots_out)
    dots_out[:, :wide] = jnp.where(at == k, row, 0.0 if dots_in is None else dots_in[:, :wide])


class Cx:
    def __init__(self, re, im):
        self.re, self.im = re, im

    def __add__(self, o):
        return Cx(self.re + o.re, self.im + o.im)

    def __sub__(self, o):
        return Cx(self.re - o.re, self.im - o.im)

    def __mul__(self, o):
        if isinstance(o, Cx):
            return Cx(self.re * o.re - self.im * o.im, self.re * o.im + self.im * o.re)
        return Cx(self.re * o, self.im * o)

    def conj(self):
        return Cx(self.re, -self.im)

    def sq(self):
        return self.re * self.re + self.im * self.im


def small_problem(gram, mu):
    steps = INNER_STEPS

    def applied(vec):
        return {j: total_of(gram[j][k] * v for k, v in vec.items()) for j in range(steps + 2)}

    def dot(left, image):
        return total_of(v.conj() * image[k] for k, v in left.items())

    def less(vec, scale, other):
        out = dict(vec)
        for k, v in other.items():
            out[k] = out[k] - scale * v if k in out else Cx(-(scale * v).re, -(scale * v).im)
        return out

    def scaled(vec, by):
        return {k: v * by for k, v in vec.items()}

    def times_operator(vec, shift):
        out = {}
        for k, v in vec.items():
            out[k + 1] = v
        for k, v in vec.items():
            out[k] = out[k] + shift * v if k in out else shift * v
        return out

    first = gram[0][0].re
    unit = 1.0 / jnp.sqrt(first + EPSILON)
    zero = jnp.zeros_like(first)
    u = {0: Cx(unit, zero)}
    u_image = applied(u)
    w = times_operator(u, mu)
    w_image = applied(w)
    image_sq = dot(w, w_image).re
    cross = dot(w, u_image)
    bottom = cross.sq()
    theta = Cx(image_sq * cross.re / bottom, -image_sq * cross.im / bottom)
    r = less(w, theta, u)
    along = dot(u, applied(r))
    b = scaled(less(r, along, u), -1.0)
    beta = jnp.sqrt(dot(b, applied(b)).re + EPSILON)
    q = [scaled(b, 1.0 / beta)]
    q_image = [applied(q[0])]
    hess = []
    shift = mu - theta
    for column in range(steps):
        z = times_operator(q[-1], shift)
        z = less(z, dot(u, applied(z)), u)
        z_image = applied(z)
        column_dots = [dot(one, z_image) for one in q]
        for value, one in zip(column_dots, q):
            z = less(z, value, one)
        z_image = applied(z)
        length = jnp.sqrt(dot(z, z_image).re + EPSILON)
        hess.append((column_dots, length))
        if column + 1 < steps:
            q.append(scaled(z, 1.0 / length))
    full = []
    for column, (dots, length) in enumerate(hess):
        entries = {i: v for i, v in enumerate(dots)}
        entries[column + 1] = Cx(length, zero)
        full.append(entries)

    def column_dot(i, j):
        return total_of(full[i][k].conj() * full[j][k] for k in full[i] if k in full[j])

    low = [[None] * steps for _ in range(steps)]
    for j in range(steps):
        diagonal = column_dot(j, j).re
        for k in range(j):
            diagonal = diagonal - low[j][k].sq()
        root = jnp.sqrt(diagonal)
        low[j][j] = root
        for i in range(j + 1, steps):
            value = column_dot(i, j)
            for k in range(j):
                value = value - low[i][k] * low[j][k].conj()
            low[i][j] = value * (1.0 / root)
    middle = []
    for i in range(steps):
        value = full[i][0].conj() * beta
        for k in range(i):
            value = value - low[i][k] * middle[k]
        middle.append(value * (1.0 / low[i][i]))
    solved = [None] * steps
    for i in reversed(range(steps)):
        value = middle[i]
        for k in range(i + 1, steps):
            value = value - low[k][i].conj() * solved[k]
        solved[i] = value * (1.0 / low[i][i])
    update = {}
    for value, one in zip(solved, q):
        for k, v in one.items():
            update[k] = update[k] + value * v if k in update else value * v
    update_sq = dot(update, applied(update)).re
    return theta, update, update_sq


def end_kernel(rows, depth, scale, shift, gram_s, gram, basis, *refs):
    powers, out, ritz, column = refs[: INNER_STEPS + 1], refs[-3], refs[-2], refs[-1]
    count = basis.shape[0]
    width = basis.shape[3]
    base = 2 * count
    tile = (8, 128)

    def splat(i, j):
        return jnp.full(tile, gram_s[i, j] * scale, jnp.float32)

    size = INNER_STEPS + 2
    table = [[None] * size for _ in range(size)]
    for i in range(size):
        for j in range(i, size):
            im = splat(j, base + 8 + i) if i != j else jnp.zeros(tile, jnp.float32)
            table[i][j] = Cx(splat(j, base + i), im)
            if i != j:
                table[j][i] = table[i][j].conj()
    mu = Cx(
        jnp.full(tile, CENTRE - shift[0], jnp.float32), jnp.full(tile, -shift[1], jnp.float32)
    )
    theta, update, update_sq = small_problem(table, mu)
    lane = lax.broadcasted_iota(jnp.int32, (1, 128), 1)
    ritz[...] = jnp.where(lane == 0, theta.re[0:1], theta.im[0:1])

    def lanes(x):
        return jnp.sum(x, axis=1, keepdims=True)

    def sublanes(x):
        return jnp.sum(x, axis=0, keepdims=True)

    def shifted(x, by):
        return pltpu.roll(x, 128 - by, 1)

    packed = gram[8:16, :] * scale
    folds = 128 // base
    whole = jnp.concatenate([packed] + [shifted(packed, base * q) for q in range(1, folds)], axis=0)
    top, bottom = whole[:count], whole[count:base]
    g_re = top + shifted(bottom, count)
    g_im = shifted(top, count) - bottom
    lane = lax.broadcasted_iota(jnp.int32, (count, 128), 1)
    same = lax.broadcasted_iota(jnp.int32, (count, 128), 0) == lane
    by_re = total_of(gram[k : k + 1, :] * v.re[0:1] for k, v in update.items()) * scale
    by_im = total_of(gram[k : k + 1, :] * v.im[0:1] for k, v in update.items()) * scale
    first_re = lanes(jnp.where(same, by_re - shifted(by_im, count), 0.0))
    first_im = lanes(jnp.where(same, by_im + shifted(by_re, count), 0.0))

    def across(col):
        return sublanes(jnp.where(same, col, 0.0))

    def mixed(col_re, col_im):
        row_re, row_im = across(col_re), across(col_im)
        return (
            lanes(g_re * row_re - g_im * row_im),
            lanes(g_re * row_im + g_im * row_re),
        )

    mixed_re, mixed_im = mixed(first_re, first_im)
    second_re, second_im = first_re - mixed_re, first_im - mixed_im
    again_re, again_im = mixed(second_re, second_im)
    change = (
        -2.0 * (first_re * first_re + first_im * first_im)
        + (first_re * mixed_re + first_im * mixed_im)
        - 2.0 * (second_re * second_re + second_im * second_im)
        + (second_re * again_re + second_im * again_im)
    )
    final_sq = update_sq[0:1, 0:1] + sublanes(change)
    inverse = 1.0 / jnp.sqrt(final_sq + EPSILON)
    column[0] = jnp.broadcast_to((first_re + second_re) * inverse, (count, 128))
    column[1] = jnp.broadcast_to((first_im + second_im) * inverse, (count, 128))
    full_inverse = jnp.broadcast_to(inverse, tile)
    coefs = {k: v * full_inverse for k, v in update.items()}

    def wide(x):
        return jnp.tile(x[0:1, :], (1, width // 128))

    coefs = {k: Cx(wide(v.re), wide(v.im)) for k, v in coefs.items()}
    for a in range(rows):
        span = slice(a * depth, (a + 1) * depth)
        real = jnp.zeros((depth, width), jnp.float32)
        imag = real
        for k, v in coefs.items():
            re, im = powers[k][0, span, :], powers[k][1, span, :]
            real = real + (v.re * re - v.im * im)
            imag = imag + (v.re * im + v.im * re)
        for i in range(count):
            v = Cx(wide(column[0, i : i + 1, :]), wide(column[1, i : i + 1, :]))
            re, im = basis[i, 0, span, :], basis[i, 1, span, :]
            real = real - (v.re * re - v.im * im)
            imag = imag - (v.re * im + v.im * re)
        out[0, span, :] = real
        out[1, span, :] = imag


def on_device(
    search_basis, coefficients, target_shift, stiffness_diag, flame_mats,
    flame_count, flame_line, flame_burner, reference_part, reference_line,
):
    n_azim, n_dom = lax.axis_size("azim"), lax.axis_size("dom")
    count, _, rows, depth, width = search_basis.shape
    lines = rows * depth
    scale = 1.0 / float(stiffness_diag.size * n_azim * n_dom)
    slots = flame_mats.shape[0]
    base = 2 * rows
    tall = base + 2 * reference_part.shape[0]
    basis = search_basis.reshape(count, 2, lines, width)
    basis_rows = search_basis.reshape(count * 2 * lines, width)
    diag = stiffness_diag.reshape(lines, width)
    mats = flame_mats.reshape(slots, 2 * width, width)

    def exchange(values, axis, pairs):
        both = pairs + [(j, i) for i, j in pairs]
        return lax.ppermute(values, axis, both)

    azim_even = [(i, i + 1) for i in range(0, n_azim, 2)]
    azim_odd = [(i, (i + 1) % n_azim) for i in range(1, n_azim, 2)]
    dom_even = [(i, i + 1) for i in range(0, n_dom, 2)]
    dom_odd = [(i, (i + 1) % n_dom) for i in range(1, n_dom, 2)]

    def shape(*dims):
        return jax.ShapeDtypeStruct(dims, jnp.float32)

    fields = [
        shape(2, lines, width),
        shape(2, depth, width),
        shape(2, depth, width),
        shape(tall, width),
        shape(tall, width),
    ]
    here = functools.partial(start_kernel, rows, depth)
    power, azim_x, azim_y, dom_x, dom_y = call(
        here, fields, smem(3) + vmem(1), (coefficients, reference_part, reference_line, basis)
    )
    powers = [power]
    held = VMEM((2 * count + 16, 128), jnp.float32)
    cross = jnp.einsum("icarl,jdarl->cidj", search_basis, search_basis, precision=HIGHEST)
    folded_gram = cross.reshape(-1, 8, 2 * count).transpose(1, 0, 2).reshape(8, 8 * count)
    is_sum = lax.broadcasted_iota(jnp.int32, (tall, width), 0) >= base
    for step in range(INNER_STEPS + 1):
        from_ay = exchange(azim_y, "azim", azim_odd)
        from_dx = exchange(dom_x, "dom", dom_even)
        dom_y = jnp.where(is_sum, dom_x + from_dx, dom_y)
        from_dy = exchange(dom_y, "dom", dom_odd)
        from_ax = exchange(azim_x, "azim", azim_even)
        sums = dom_y + from_dy
        reach = 4
        while reach < n_dom:
            pairs = [(i, i ^ reach) for i in range(n_dom) if i < i ^ reach]
            sums = sums + exchange(sums, "dom", pairs)
            reach *= 2
        given = (mats, sums, basis, *powers, *([dots] if step else []))
        flame, dots = call(
            functools.partial(flame_kernel, base, step),
            [shape(2, lines, width), shape(8, 128)],
            smem(3) + vmem(len(given)),
            (flame_count, flame_line, flame_burner, *given),
            [VMEM((reference_part.shape[0], 16, width), jnp.bfloat16), held],
        )
        received = (power, flame, diag, from_ax, from_ay, from_dx, from_dy)
        if step < INNER_STEPS:
            power, azim_x, azim_y, dom_x, dom_y = call(
                functools.partial(step_kernel, rows, depth),
                fields,
                smem(2) + vmem(7),
                (reference_part, reference_line, *received),
            )
        else:
            dots = call(
                functools.partial(last_kernel, rows, depth),
                shape(8, 128),
                vmem(8 + len(powers)),
                (*received, *powers, dots),
                [VMEM((2, lines, width), jnp.float32), held],
            )
        powers.append(power)
    devices = n_azim * n_dom
    packed = jnp.concatenate([dots, folded_gram], axis=0)
    spread = jnp.broadcast_to(packed[None], (devices, *packed.shape))
    gram = jnp.sum(lax.all_to_all(spread, ("azim", "dom"), 0, 0), axis=0)
    new_vector, ritz = call(
        functools.partial(end_kernel, rows, depth, scale),
        [shape(2, lines, width), shape(1, 128)],
        smem(2) + vmem(2 + INNER_STEPS + 1),
        (target_shift, gram, gram, basis, *powers[: INNER_STEPS + 1]),
        [VMEM((2, count, 128), jnp.float32)],
    )
    return new_vector.reshape(2, rows, depth, width), ritz[0, :2]


def solution(mesh):
    placed = (
        P(None, None, "azim", "dom", None),
        P(),
        P(),
        P("azim", "dom", None),
        P(("azim", "dom"), None, None, None),
        P(("azim", "dom")),
        P(("azim", "dom")),
        P(("azim", "dom")),
        P("azim"),
        P("azim"),
    )
    return jax.shard_map(
        on_device,
        mesh=mesh,
        in_specs=placed,
        out_specs=(P(None, "azim", "dom", None), P()),
        check_vma=False,
    )
```

```python
import functools

import jax
import jax.numpy as jnp
from jax import lax
from jax.experimental import pallas as pl
from jax.experimental.pallas import tpu as pltpu
from jax.sharding import PartitionSpec as P

INNER_STEPS = 3
EPSILON = 1e-06
CENTRE = 7.125
PARTS = 2
START_LIMIT = 61 << 20
HIGHEST = lax.Precision.HIGHEST
VMEM = pltpu.VMEM
SMEM = pltpu.SMEM


def vmem(count):
    return [pl.BlockSpec(memory_space=VMEM) for _ in range(count)]


def smem(count):
    return [pl.BlockSpec(memory_space=SMEM) for _ in range(count)]


def in_hbm(count):
    return [pl.BlockSpec(memory_space=pltpu.HBM) for _ in range(count)]


def call(kernel, outs, specs, args, scratch=(), cost=1, out_specs=None, limit=8 << 20):
    estimate = pl.CostEstimate(flops=0, transcendentals=0, bytes_accessed=cost * 2_000_000)
    if out_specs is None:
        out_specs = jax.tree.map(lambda _: pl.BlockSpec(memory_space=VMEM), outs)
    return pl.pallas_call(
        kernel,
        out_shape=outs,
        in_specs=specs,
        out_specs=out_specs,
        scratch_shapes=list(scratch),
        compiler_params=pltpu.CompilerParams(vmem_limit_bytes=limit),
        cost_estimate=estimate,
    )(*args)


def write_edges(rows, depth, field, ref_part, ref_line, azim_x, azim_y, dom_x, dom_y):
    odd_a = lax.axis_index("azim") % 2
    part = lax.axis_index("dom")
    odd_d = part % 2
    last = (rows - 1) * depth
    x_start = pl.multiple_of((1 - odd_a) * last, depth)
    y_start = pl.multiple_of(odd_a * last, depth)
    for c in range(2):
        azim_x[c] = field[c, pl.ds(x_start, depth), :]
        azim_y[c] = field[c, pl.ds(y_start, depth), :]
        for a in range(rows):
            x_row = a * depth + (1 - odd_d) * (depth - 1)
            y_row = a * depth + odd_d * (depth - 1)
            at = c * rows + a
            dom_x[at : at + 1, :] = field[c, pl.ds(x_row, 1), :]
            dom_y[at : at + 1, :] = field[c, pl.ds(y_row, 1), :]
    base = 2 * rows
    for b in range((dom_x.shape[0] - base) // 2):
        mine = ref_part[b] == part
        for c in range(2):
            at = base + 2 * b + c
            line = field[c, pl.ds(ref_line[b], 1), :]
            dom_x[at : at + 1, :] = jnp.where(mine, line, 0.0)
            dom_y[at : at + 1, :] = jnp.zeros_like(line)


def start_kernel(
    rows, depth, small, basis_in, field, azim_x, azim_y, dom_x, dom_y, basis, sems
):
    count = basis.shape[0]
    copies = [pltpu.make_async_copy(basis_in.at[i], basis.at[i], sems.at[i]) for i in range(count)]
    for copy in copies:
        copy.start()
    for i in range(count):
        copies[i].wait()
        one, two = small[i], small[count + i]
        for a in range(rows):
            span = slice(a * depth, (a + 1) * depth)
            re, im = basis[i, 0, span, :], basis[i, 1, span, :]
            real = one * re - two * im
            imag = one * im + two * re
            field[0, span, :] = real if i == 0 else field[0, span, :] + real
            field[1, span, :] = imag if i == 0 else field[1, span, :] + imag
    burners = (small.shape[0] - 2 * count) // 2
    numbers = [small[2 * count + i].astype(jnp.int32) for i in range(2 * burners)]
    write_edges(
        rows, depth, field, numbers[:burners], numbers[burners:], azim_x, azim_y, dom_x, dom_y
    )


def basis_kernel(part, parts, basis, out, tiles):
    half = basis.shape[0]
    count = 2 * half
    lines, width = basis.shape[2] // parts, basis.shape[3]
    first = part * lines
    for c in range(2):
        for i in range(half):
            for j in range(width // 128):
                at = (c * half + i) * lines
                tiles[j, at : at + lines, :] = basis[
                    i, c, first : first + lines, j * 128 : (j + 1) * 128
                ]

    def one(line):
        tall = jnp.concatenate(
            [tiles.at[j][pl.ds(line, count, stride=lines), :] for j in range(width // 128)], axis=1
        )
        high = tall.astype(jnp.bfloat16)
        low = (tall - high.astype(jnp.float32)).astype(jnp.bfloat16)
        return jnp.concatenate([high, low], axis=0)

    group = 4

    def some(at, total):
        both = jnp.concatenate([one(at * group + i) for i in range(group)], axis=1)
        return total + lax.dot_general(
            both, both, (((1,), (1,)), ((), ())), preferred_element_type=jnp.float32
        )

    zero = jnp.zeros((2 * count, 2 * count), jnp.float32)
    total = lax.fori_loop(0, lines // group, some, zero)
    total = total[:count] + total[count:]
    total = jnp.concatenate([total, jnp.zeros((count, 128 - 2 * count), jnp.float32)], axis=1)
    total = total + pltpu.roll(total, 128 - count, 1)
    top, bottom = total[:half], total[half:]
    crossed = pltpu.roll(top, 128 - half, 1)
    lane = lax.broadcasted_iota(jnp.int32, (half, 128), 1)
    table = jnp.where(
        lane < half, top + pltpu.roll(bottom, 128 - half, 1) + crossed - bottom, 0.0
    )
    out[...] = jnp.zeros_like(out)
    folds = 128 // half
    for r in range(half // folds):
        rows = [
            pltpu.roll(table[r * folds + s : r * folds + s + 1], half * s, 1) if s
            else table[r * folds : r * folds + 1]
            for s in range(folds)
        ]
        out[5 + r : 6 + r, :] = total_of(rows)


def dots_kernel(k, basis, *refs):
    powers, (dots_out, held) = refs[: k + 1], refs[-2:]
    dots_in = refs[k + 1] if k else None
    add_dots(k, basis, powers[:-1], powers[-1], dots_in, dots_out, held)


def flame_kernel(base, live, lines, burners, mats, sums, *refs):
    out, source = refs[-2:]
    width = sums.shape[1]
    slots = mats.shape[0]
    rows = sums.shape[0] - base
    source[...] = jnp.zeros_like(source)
    for i in range(rows):
        row = sums[base + i : base + i + 1, :]
        high = row.astype(jnp.bfloat16)
        source[2 * i : 2 * i + 1, :] = high
        source[2 * i + 1 : 2 * i + 2, :] = (row - high.astype(jnp.float32)).astype(jnp.bfloat16)
    out[...] = jnp.zeros_like(out)
    left = source[...]

    def products(blocks):
        return lax.dot_general(
            left, blocks, (((1,), (1,)), ((), ())), preferred_element_type=jnp.float32
        )

    def put(s, product):
        chosen = product[0:4]
        for b in range(1, rows // 2):
            chosen = jnp.where(burners[s] == b, product[4 * b : 4 * b + 4], chosen)
        by_re = chosen[0:1] + chosen[1:2]
        by_im = chosen[2:3] + chosen[3:4]
        at = pl.ds(lines[s], 1)
        out[0, at, :] += by_re[:, :width] - by_im[:, width:]
        out[1, at, :] += by_im[:, :width] + by_re[:, width:]

    few = 2

    @pl.when(live[0] <= few)
    def _():
        def slot(s, carry):
            put(s, products(mats[s]))
            return carry

        lax.fori_loop(0, live[0], slot, 0)

    @pl.when(live[0] > few)
    def _():
        every = products(mats[...].reshape(slots * 2 * width, width))
        for s in range(slots):

            @pl.when(s < live[0])
            def _():
                put(s, every[:, 2 * width * s : 2 * width * (s + 1)])


def step_kernel(
    rows, depth, ref_part, ref_line, old, flame, diag, from_ax, from_ay, from_dx, from_dy,
    field, azim_x, azim_y, dom_x, dom_y,
):
    width = old.shape[2]
    odd_a = lax.axis_index("azim") % 2 == 1
    part = lax.axis_index("dom")
    odd_d = part % 2 == 1
    row_at = lax.broadcasted_iota(jnp.int32, (depth, width), 0)
    lane_at = lax.broadcasted_iota(jnp.int32, (depth, width), 1)
    for c in range(2):
        before = jnp.where(odd_a, from_ax[c], from_ay[c])
        after = jnp.where(odd_a, from_ay[c], from_ax[c])
        planes = [old[c, a * depth : (a + 1) * depth, :] for a in range(rows)]
        around = [before, *planes, after]
        for a in range(rows):
            here = planes[a]
            at = c * rows + a
            one, two = from_dx[at : at + 1, :], from_dy[at : at + 1, :]
            inner = jnp.where(part == 0, 0.0, jnp.where(odd_d, one, two))
            outer = jnp.where(part == lax.axis_size("dom") - 1, 0.0, jnp.where(odd_d, two, one))
            down = jnp.where(row_at == 0, inner, pltpu.roll(here, 1, 0))
            up = jnp.where(row_at == depth - 1, outer, pltpu.roll(here, depth - 1, 0))
            left = jnp.where(lane_at == 0, 0.0, pltpu.roll(here, 1, 1))
            right = jnp.where(lane_at == width - 1, 0.0, pltpu.roll(here, width - 1, 1))
            beside = (around[a] + around[a + 2]) + (down + up) + (left + right)
            span = slice(a * depth, (a + 1) * depth)
            factor = diag[span, :] + (6.0 - CENTRE)
            field[c, span, :] = factor * here - beside + flame[c, span, :]
    if azim_x is not None:
        write_edges(rows, depth, field, ref_part, ref_line, azim_x, azim_y, dom_x, dom_y)


def last_kernel(rows, depth, *refs):
    first, tables, powers = refs[:7], refs[7 : 7 + PARTS], refs[7 + PARTS : -4]
    dots_in, dots_out, field, held = refs[-4:]
    step_kernel(rows, depth, None, None, *first, field, None, None, None, None)
    add_dots(len(powers), None, powers, field, dots_in, dots_out, held)
    dots_out[...] += total_of(table[...] for table in tables)


def folded(x):
    tall = total_of(x[i : i + 8] for i in range(0, x.shape[0], 8))
    tile = total_of(tall[:, j : j + 128] for j in range(0, x.shape[1], 128))
    return jnp.sum(tile, axis=0, keepdims=True)


def total_of(terms):
    terms = list(terms)
    while len(terms) > 1:
        terms = [
            terms[i] + terms[i + 1] if i + 1 < len(terms) else terms[i]
            for i in range(0, len(terms), 2)
        ]
    return terms[0]


def add_dots(k, basis, powers, current, dots_in, dots_out, held):
    held[...] = jnp.zeros_like(held)
    re, im = current[0], current[1]
    count = 0
    if basis is not None:
        count = basis.shape[0]

        def one(i, carry):
            left_re, left_im = basis[i, 0], basis[i, 1]
            held[pl.ds(i, 1), :] = folded(left_re * re + left_im * im)
            held[pl.ds(count + i, 1), :] = folded(left_re * im - left_im * re)
            return carry

        lax.fori_loop(0, count, one, 0)
    first = held.shape[0] - 16
    for j, power in enumerate([*powers, current]):
        left_re, left_im = power[0], power[1]
        held[first + j : first + j + 1, :] = folded(left_re * re + left_im * im)
        held[first + 8 + j : first + 9 + j, :] = folded(left_re * im - left_im * re)
    row = lax.dot_general(
        jnp.ones((8, 128), jnp.float32), held[...], (((1,), (1,)), ((), ())),
        precision=HIGHEST, preferred_element_type=jnp.float32,
    )
    at = lax.broadcasted_iota(jnp.int32, row.shape, 0)
    wide = row.shape[1]
    dots_out[...] = jnp.zeros_like(dots_out)
    dots_out[:, :wide] = jnp.where(at == k, row, 0.0 if dots_in is None else dots_in[:, :wide])


class Cx:
    def __init__(self, re, im):
        self.re, self.im = re, im

    def __add__(self, o):
        return Cx(self.re + o.re, self.im + o.im)

    def __sub__(self, o):
        return Cx(self.re - o.re, self.im - o.im)

    def __mul__(self, o):
        if isinstance(o, Cx):
            return Cx(self.re * o.re - self.im * o.im, self.re * o.im + self.im * o.re)
        return Cx(self.re * o, self.im * o)

    def conj(self):
        return Cx(self.re, -self.im)

    def sq(self):
        return self.re * self.re + self.im * self.im


def small_problem(gram, mu):
    steps = INNER_STEPS

    def applied(vec):
        return {j: total_of(gram[j][k] * v for k, v in vec.items()) for j in range(steps + 2)}

    def dot(left, image):
        return total_of(v.conj() * image[k] for k, v in left.items())

    def less(vec, scale, other):
        out = dict(vec)
        for k, v in other.items():
            out[k] = out[k] - scale * v if k in out else Cx(-(scale * v).re, -(scale * v).im)
        return out

    def scaled(vec, by):
        return {k: v * by for k, v in vec.items()}

    def times_operator(vec, shift):
        out = {}
        for k, v in vec.items():
            out[k + 1] = v
        for k, v in vec.items():
            out[k] = out[k] + shift * v if k in out else shift * v
        return out

    first = gram[0][0].re
    unit = 1.0 / jnp.sqrt(first + EPSILON)
    zero = jnp.zeros_like(first)
    u = {0: Cx(unit, zero)}
    u_image = applied(u)
    w = times_operator(u, mu)
    w_image = applied(w)
    image_sq = dot(w, w_image).re
    cross = dot(w, u_image)
    bottom = cross.sq()
    theta = Cx(image_sq * cross.re / bottom, -image_sq * cross.im / bottom)
    r = less(w, theta, u)
    along = dot(u, applied(r))
    b = scaled(less(r, along, u), -1.0)
    beta = jnp.sqrt(dot(b, applied(b)).re + EPSILON)
    q = [scaled(b, 1.0 / beta)]
    q_image = [applied(q[0])]
    hess = []
    shift = mu - theta
    for column in range(steps):
        z = times_operator(q[-1], shift)
        z = less(z, dot(u, applied(z)), u)
        z_image = applied(z)
        column_dots = [dot(one, z_image) for one in q]
        for value, one in zip(column_dots, q):
            z = less(z, value, one)
        z_image = applied(z)
        length = jnp.sqrt(dot(z, z_image).re + EPSILON)
        hess.append((column_dots, length))
        if column + 1 < steps:
            q.append(scaled(z, 1.0 / length))
    full = []
    for column, (dots, length) in enumerate(hess):
        entries = {i: v for i, v in enumerate(dots)}
        entries[column + 1] = Cx(length, zero)
        full.append(entries)

    def column_dot(i, j):
        return total_of(full[i][k].conj() * full[j][k] for k in full[i] if k in full[j])

    low = [[None] * steps for _ in range(steps)]
    for j in range(steps):
        diagonal = column_dot(j, j).re
        for k in range(j):
            diagonal = diagonal - low[j][k].sq()
        root = jnp.sqrt(diagonal)
        low[j][j] = root
        for i in range(j + 1, steps):
            value = column_dot(i, j)
            for k in range(j):
                value = value - low[i][k] * low[j][k].conj()
            low[i][j] = value * (1.0 / root)
    middle = []
    for i in range(steps):
        value = full[i][0].conj() * beta
        for k in range(i):
            value = value - low[i][k] * middle[k]
        middle.append(value * (1.0 / low[i][i]))
    solved = [None] * steps
    for i in reversed(range(steps)):
        value = middle[i]
        for k in range(i + 1, steps):
            value = value - low[k][i].conj() * solved[k]
        solved[i] = value * (1.0 / low[i][i])
    update = {}
    for value, one in zip(solved, q):
        for k, v in one.items():
            update[k] = update[k] + value * v if k in update else value * v
    update_sq = dot(update, applied(update)).re
    return theta, update, update_sq


def end_kernel(rows, depth, scale, shift, gram_s, gram, basis, *refs):
    powers, out, ritz, column = refs[: INNER_STEPS + 1], refs[-3], refs[-2], refs[-1]
    count = basis.shape[0]
    width = basis.shape[3]
    base = 2 * count
    tile = (8, 128)

    def splat(i, j):
        return jnp.full(tile, gram_s[i, j] * scale, jnp.float32)

    size = INNER_STEPS + 2
    table = [[None] * size for _ in range(size)]
    for i in range(size):
        for j in range(i, size):
            im = splat(j, base + 8 + i) if i != j else jnp.zeros(tile, jnp.float32)
            table[i][j] = Cx(splat(j, base + i), im)
            if i != j:
                table[j][i] = table[i][j].conj()
    mu = Cx(
        jnp.full(tile, CENTRE - shift[0], jnp.float32), jnp.full(tile, -shift[1], jnp.float32)
    )
    theta, update, update_sq = small_problem(table, mu)
    ritz[0] = theta.re[0, 0]
    ritz[1] = theta.im[0, 0]

    def lanes(x):
        return jnp.sum(x, axis=1, keepdims=True)

    def sublanes(x):
        return jnp.sum(x, axis=0, keepdims=True)

    def shifted(x, by):
        return pltpu.roll(x, 128 - by, 1)

    folds = 128 // count
    table = jnp.concatenate(
        [
            shifted(gram[5 + r : 6 + r, :], count * q) if q else gram[5 + r : 6 + r, :]
            for r in range(count // folds)
            for q in range(folds)
        ],
        axis=0,
    )
    lane = lax.broadcasted_iota(jnp.int32, (count, 128), 1)
    same = lax.broadcasted_iota(jnp.int32, (count, 128), 0) == lane
    by_re = total_of(gram[k : k + 1, :] * v.re[0:1] for k, v in update.items()) * scale
    by_im = total_of(gram[k : k + 1, :] * v.im[0:1] for k, v in update.items()) * scale
    first_re = lanes(jnp.where(same, by_re - shifted(by_im, count), 0.0))
    first_im = lanes(jnp.where(same, by_im + shifted(by_re, count), 0.0))

    table = jnp.where(lane < count, table, 0.0) * (0.5 * scale)

    def across(col):
        return sublanes(jnp.where(same, col, 0.0))

    def mixed(col_re, col_im):
        def halves(col):
            straight = lanes(table * across(col))
            turned = lanes(jnp.where(same, sublanes(table * col), 0.0))
            return straight + turned, straight - turned

        re_re, im_re = halves(col_re)
        re_im, im_im = halves(col_im)
        return re_re - im_im, re_im + im_re

    mixed_re, mixed_im = mixed(first_re, first_im)
    second_re, second_im = first_re - mixed_re, first_im - mixed_im
    again_re, again_im = mixed(second_re, second_im)
    change = (
        -2.0 * (first_re * first_re + first_im * first_im)
        + (first_re * mixed_re + first_im * mixed_im)
        - 2.0 * (second_re * second_re + second_im * second_im)
        + (second_re * again_re + second_im * again_im)
    )
    final_sq = update_sq[0:1, 0:1] + sublanes(change)
    inverse = 1.0 / jnp.sqrt(final_sq + EPSILON)
    column[0] = jnp.broadcast_to((first_re + second_re) * inverse, (count, 128))
    column[1] = jnp.broadcast_to((first_im + second_im) * inverse, (count, 128))
    full_inverse = jnp.broadcast_to(inverse, tile)
    coefs = {k: v * full_inverse for k, v in update.items()}

    def wide(x):
        return jnp.tile(x[0:1, :], (1, width // 128))

    coefs = {k: Cx(wide(v.re), wide(v.im)) for k, v in coefs.items()}
    for a in range(rows):
        span = slice(a * depth, (a + 1) * depth)
        real = jnp.zeros((depth, width), jnp.float32)
        imag = real
        for k, v in coefs.items():
            re, im = powers[k][0, span, :], powers[k][1, span, :]
            real = real + (v.re * re - v.im * im)
            imag = imag + (v.re * im + v.im * re)
        for i in range(count):
            v = Cx(wide(column[0, i : i + 1, :]), wide(column[1, i : i + 1, :]))
            re, im = basis[i, 0, span, :], basis[i, 1, span, :]
            real = real - (v.re * re - v.im * im)
            imag = imag - (v.re * im + v.im * re)
        out[0, span, :] = real
        out[1, span, :] = imag


def on_device(
    search_basis, coefficients, target_shift, stiffness_diag, flame_mats,
    flame_count, flame_line, flame_burner, reference_part, reference_line,
):
    n_azim, n_dom = lax.axis_size("azim"), lax.axis_size("dom")
    count, _, rows, depth, width = search_basis.shape
    lines = rows * depth
    scale = 1.0 / float(stiffness_diag.size * n_azim * n_dom)
    slots = flame_mats.shape[0]
    base = 2 * rows
    tall = base + 2 * reference_part.shape[0]
    basis = search_basis.reshape(count, 2, lines, width)
    diag = stiffness_diag.reshape(lines, width)
    mats = flame_mats.reshape(slots, 2 * width, width)

    def exchange(values, axis, pairs):
        both = pairs + [(j, i) for i, j in pairs]
        return lax.ppermute(values, axis, both)

    azim_even = [(i, i + 1) for i in range(0, n_azim, 2)]
    azim_odd = [(i, (i + 1) % n_azim) for i in range(1, n_azim, 2)]
    dom_even = [(i, i + 1) for i in range(0, n_dom, 2)]
    dom_odd = [(i, (i + 1) % n_dom) for i in range(1, n_dom, 2)]

    def shape(*dims):
        return jax.ShapeDtypeStruct(dims, jnp.float32)

    fields = [
        shape(2, lines, width),
        shape(2, depth, width),
        shape(2, depth, width),
        shape(tall, width),
        shape(tall, width),
    ]
    small = jnp.concatenate(
        [
            coefficients.reshape(-1),
            reference_part.astype(jnp.float32),
            reference_line.astype(jnp.float32),
        ]
    )
    power, azim_x, azim_y, dom_x, dom_y, basis = call(
        functools.partial(start_kernel, rows, depth),
        [*fields, shape(count, 2, lines, width)],
        smem(1) + in_hbm(1),
        (small, basis),
        [pltpu.SemaphoreType.DMA((count,))],
        cost=4,
        limit=START_LIMIT,
    )
    powers = [power]
    held = VMEM((2 * count + 16, 128), jnp.float32)
    tables = [
        call(
            functools.partial(basis_kernel, part, PARTS),
            shape(8, 128),
            vmem(1),
            (basis,),
            [VMEM((width // 128, count * 2 * (lines // PARTS), 128), jnp.float32)],
        )
        for part in range(PARTS)
    ]
    is_sum = lax.broadcasted_iota(jnp.int32, (tall, width), 0) >= base
    for step in range(INNER_STEPS + 1):
        from_ay = exchange(azim_y, "azim", azim_odd)
        from_dx = exchange(dom_x, "dom", dom_even)
        dom_y = jnp.where(is_sum, dom_x + from_dx, dom_y)
        from_dy = exchange(dom_y, "dom", dom_odd)
        from_ax = exchange(azim_x, "azim", azim_even)
        sums = dom_y + from_dy
        reach = 4
        while reach < n_dom:
            pairs = [(i, i ^ reach) for i in range(n_dom) if i < i ^ reach]
            sums = sums + exchange(sums, "dom", pairs)
            reach *= 2
        given = (basis, *powers, *([dots] if step else []))
        dots = call(
            functools.partial(dots_kernel, step), shape(8, 128), vmem(len(given)), given, [held]
        )
        order = (dots, *tables[step - 1 : step]) if step else (dots,)
        flame = call(
            functools.partial(flame_kernel, base),
            shape(2, lines, width),
            smem(3) + vmem(2 + len(order)),
            (flame_count, flame_line, flame_burner, mats, sums, *order),
            [VMEM((16, width), jnp.bfloat16)],
            cost=3,
        )
        received = (power, flame, diag, from_ax, from_ay, from_dx, from_dy)
        if step < INNER_STEPS:
            power, azim_x, azim_y, dom_x, dom_y = call(
                functools.partial(step_kernel, rows, depth),
                fields,
                smem(2) + vmem(7),
                (reference_part, reference_line, *received),
            )
        else:
            dots = call(
                functools.partial(last_kernel, rows, depth),
                shape(8, 128),
                vmem(8 + len(tables) + len(powers)),
                (*received, *tables, *powers, dots),
                [VMEM((2, lines, width), jnp.float32), held],
            )
        powers.append(power)
    devices = n_azim * n_dom
    spread = jnp.broadcast_to(dots[None], (devices, *dots.shape))
    gram = jnp.sum(lax.all_to_all(spread, ("azim", "dom"), 0, 0), axis=0)
    new_vector, ritz = call(
        functools.partial(end_kernel, rows, depth, scale),
        [shape(2, lines, width), shape(2)],
        smem(2) + vmem(2 + INNER_STEPS + 1),
        (target_shift, gram, gram, basis, *powers[: INNER_STEPS + 1]),
        [VMEM((2, count, 128), jnp.float32)],
        out_specs=[pl.BlockSpec(memory_space=VMEM), pl.BlockSpec(memory_space=SMEM)],
    )
    return new_vector.reshape(2, rows, depth, width), ritz


def solution(mesh):
    placed = (
        P(None, None, "azim", "dom", None),
        P(),
        P(),
        P("azim", "dom", None),
        P(("azim", "dom"), None, None, None),
        P(("azim", "dom")),
        P(("azim", "dom")),
        P(("azim", "dom")),
        P("azim"),
        P("azim"),
    )
    return jax.shard_map(
        on_device,
        mesh=mesh,
        in_specs=placed,
        out_specs=(P(None, "azim", "dom", None), P()),
        check_vma=False,
    )
```

```python
import functools

import jax
import jax.numpy as jnp
from jax import lax
from jax.experimental import pallas as pl
from jax.experimental.pallas import tpu as pltpu
from jax.sharding import PartitionSpec as P

INNER_STEPS = 3
EPSILON = 1e-06
CENTRE = 7.125
PARTS = 2
HIGHEST = lax.Precision.HIGHEST
VMEM = pltpu.VMEM
SMEM = pltpu.SMEM


def vmem(count):
    return [pl.BlockSpec(memory_space=VMEM) for _ in range(count)]


def smem(count):
    return [pl.BlockSpec(memory_space=SMEM) for _ in range(count)]


def in_hbm(count):
    return [pl.BlockSpec(memory_space=pltpu.HBM) for _ in range(count)]


def held_in_hbm(*arrays):
    return [pltpu.with_memory_space_constraint(a, pltpu.HBM) for a in arrays]


def call(kernel, outs, specs, args, scratch=(), cost=1, out_specs=None, limit=8 << 20):
    estimate = pl.CostEstimate(flops=0, transcendentals=0, bytes_accessed=cost * 2_000_000)
    if out_specs is None:
        out_specs = jax.tree.map(lambda _: pl.BlockSpec(memory_space=VMEM), outs)
    return pl.pallas_call(
        kernel,
        out_shape=outs,
        in_specs=specs,
        out_specs=out_specs,
        scratch_shapes=list(scratch),
        compiler_params=pltpu.CompilerParams(vmem_limit_bytes=limit),
        cost_estimate=estimate,
    )(*args)


def write_edges(rows, depth, field, ref_part, ref_line, azim_x, azim_y, dom_x, dom_y):
    odd_a = lax.axis_index("azim") % 2
    part = lax.axis_index("dom")
    odd_d = part % 2
    last = (rows - 1) * depth
    x_start = pl.multiple_of((1 - odd_a) * last, depth)
    y_start = pl.multiple_of(odd_a * last, depth)
    for c in range(2):
        azim_x[c] = field[c, pl.ds(x_start, depth), :]
        azim_y[c] = field[c, pl.ds(y_start, depth), :]
        for a in range(rows):
            x_row = a * depth + (1 - odd_d) * (depth - 1)
            y_row = a * depth + odd_d * (depth - 1)
            at = c * rows + a
            dom_x[at : at + 1, :] = field[c, pl.ds(x_row, 1), :]
            dom_y[at : at + 1, :] = field[c, pl.ds(y_row, 1), :]
    base = 2 * rows
    for b in range(ref_part.shape[0]):
        mine = ref_part[b] == part
        for c in range(2):
            at = base + 2 * b + c
            line = field[c, pl.ds(ref_line[b], 1), :]
            dom_x[at : at + 1, :] = jnp.where(mine, line, 0.0)
            dom_y[at : at + 1, :] = jnp.zeros_like(line)


def start_kernel(
    rows, depth, coef_in, part_in, line_in, basis_in,
    field, azim_x, azim_y, dom_x, dom_y, basis, coef, ref_part, ref_line, small_sems, sems,
):
    count = basis.shape[0]
    pairs = ((coef_in, coef), (part_in, ref_part), (line_in, ref_line))
    small = [pltpu.make_async_copy(a, b, small_sems.at[i]) for i, (a, b) in enumerate(pairs)]
    group = count // sems.shape[0]
    large = [
        pltpu.make_async_copy(
            basis_in.at[pl.ds(i * group, group)], basis.at[pl.ds(i * group, group)], sems.at[i]
        )
        for i in range(sems.shape[0])
    ]
    for copy in small + large:
        copy.start()
    for copy in small:
        copy.wait()
    for at, copy in enumerate(large):
        copy.wait()
        for a in range(rows):
            span = slice(a * depth, (a + 1) * depth)
            real = imag = None
            for i in range(at * group, (at + 1) * group):
                re, im = basis[i, 0, span, :], basis[i, 1, span, :]
                one = coef[0, i] * re - coef[1, i] * im
                two = coef[0, i] * im + coef[1, i] * re
                real = one if real is None else real + one
                imag = two if imag is None else imag + two
            field[0, span, :] = real if at == 0 else field[0, span, :] + real
            field[1, span, :] = imag if at == 0 else field[1, span, :] + imag
    write_edges(rows, depth, field, ref_part, ref_line, azim_x, azim_y, dom_x, dom_y)


def basis_kernel(part, parts, basis, out, tiles):
    half = basis.shape[0]
    count = 2 * half
    lines, width = basis.shape[2] // parts, basis.shape[3]
    first = part * lines
    for c in range(2):
        for i in range(half):
            for j in range(width // 128):
                at = (c * half + i) * lines
                tiles[j, at : at + lines, :] = basis[
                    i, c, first : first + lines, j * 128 : (j + 1) * 128
                ]

    def one(line):
        tall = jnp.concatenate(
            [tiles.at[j][pl.ds(line, count, stride=lines), :] for j in range(width // 128)], axis=1
        )
        high = tall.astype(jnp.bfloat16)
        low = (tall - high.astype(jnp.float32)).astype(jnp.bfloat16)
        return jnp.concatenate([high, low], axis=0)

    group = 4

    def some(at, total):
        both = jnp.concatenate([one(at * group + i) for i in range(group)], axis=1)
        return total + lax.dot_general(
            both, both, (((1,), (1,)), ((), ())), preferred_element_type=jnp.float32
        )

    zero = jnp.zeros((2 * count, 2 * count), jnp.float32)
    total = lax.fori_loop(0, lines // group, some, zero)
    total = total[:count] + total[count:]
    total = jnp.concatenate([total, jnp.zeros((count, 128 - 2 * count), jnp.float32)], axis=1)
    total = total + pltpu.roll(total, 128 - count, 1)
    top, bottom = total[:half], total[half:]
    crossed = pltpu.roll(top, 128 - half, 1)
    lane = lax.broadcasted_iota(jnp.int32, (half, 128), 1)
    table = jnp.where(
        lane < half, top + pltpu.roll(bottom, 128 - half, 1) + crossed - bottom, 0.0
    )
    out[...] = jnp.zeros_like(out)
    folds = 128 // half
    for r in range(half // folds):
        rows = [
            pltpu.roll(table[r * folds + s : r * folds + s + 1], half * s, 1) if s
            else table[r * folds : r * folds + 1]
            for s in range(folds)
        ]
        out[5 + r : 6 + r, :] = total_of(rows)


def dots_kernel(k, basis, *refs):
    powers, (dots_out, held) = refs[: k + 1], refs[-2:]
    dots_in = refs[k + 1] if k else None
    add_dots(k, basis, powers[:-1], powers[-1], dots_in, dots_out, held)


def first_dots_kernel(basis, power, mats_in, dots_out, mats, held, sems):
    half = mats.shape[0]
    copies = [pltpu.make_async_copy(mats_in.at[s], mats.at[s], sems.at[s]) for s in range(half)]
    for copy in copies:
        copy.start()
    add_dots(0, basis, [], power, None, dots_out, held)
    for copy in copies:
        copy.wait()


def flame_kernel(base, live, lines, burners, sums, lower, upper, *refs, ready=None):
    out, source = refs[-2:]
    width = sums.shape[1]
    half = lower.shape[0]
    rows = sums.shape[0] - base
    source[...] = jnp.zeros_like(source)
    for i in range(rows):
        row = sums[base + i : base + i + 1, :]
        high = row.astype(jnp.bfloat16)
        source[2 * i : 2 * i + 1, :] = high
        source[2 * i + 1 : 2 * i + 2, :] = (row - high.astype(jnp.float32)).astype(jnp.bfloat16)
    out[...] = jnp.zeros_like(out)
    left = source[...]

    def products(blocks):
        return lax.dot_general(
            left, blocks, (((1,), (1,)), ((), ())), preferred_element_type=jnp.float32
        )

    def put(s, product):
        chosen = product[0:4]
        for b in range(1, rows // 2):
            chosen = jnp.where(burners[s] == b, product[4 * b : 4 * b + 4], chosen)
        by_re = chosen[0:1] + chosen[1:2]
        by_im = chosen[2:3] + chosen[3:4]
        at = pl.ds(lines[s], 1)
        out[0, at, :] += by_re[:, :width] - by_im[:, width:]
        out[1, at, :] += by_im[:, :width] + by_re[:, width:]

    def put_all(first, blocks):
        every = products(blocks[...].reshape(half * 2 * width, width))
        for s in range(half):

            @pl.when(first + s < live[0])
            def _():
                put(first + s, every[:, 2 * width * s : 2 * width * (s + 1)])

    few = half // 2

    @pl.when(live[0] <= few)
    def _():
        def slot(s, carry):
            put(s, products(lower[s]))
            return carry

        lax.fori_loop(0, live[0], slot, 0)

    @pl.when(live[0] > few)
    def _():
        put_all(0, lower)

    if ready is not None:
        ready()

    @pl.when(live[0] > half)
    def _():
        put_all(half, upper)


def first_flame_kernel(base, live, lines, burners, sums, lower, mats_in, order, out, upper, *refs):
    source, sems = refs
    half = lower.shape[0]
    copies = [
        pltpu.make_async_copy(mats_in.at[half + s], upper.at[s], sems.at[s]) for s in range(half)
    ]
    for copy in copies:
        copy.start()

    def ready():
        for copy in copies:
            copy.wait()

    flame_kernel(base, live, lines, burners, sums, lower, upper, order, out, source, ready=ready)


def step_kernel(
    rows, depth, ref_part, ref_line, old, flame, diag, from_ax, from_ay, from_dx, from_dy,
    field, azim_x, azim_y, dom_x, dom_y,
):
    width = old.shape[2]
    odd_a = lax.axis_index("azim") % 2 == 1
    part = lax.axis_index("dom")
    odd_d = part % 2 == 1
    row_at = lax.broadcasted_iota(jnp.int32, (depth, width), 0)
    lane_at = lax.broadcasted_iota(jnp.int32, (depth, width), 1)
    for c in range(2):
        before = jnp.where(odd_a, from_ax[c], from_ay[c])
        after = jnp.where(odd_a, from_ay[c], from_ax[c])
        planes = [old[c, a * depth : (a + 1) * depth, :] for a in range(rows)]
        around = [before, *planes, after]
        for a in range(rows):
            here = planes[a]
            at = c * rows + a
            one, two = from_dx[at : at + 1, :], from_dy[at : at + 1, :]
            inner = jnp.where(part == 0, 0.0, jnp.where(odd_d, one, two))
            outer = jnp.where(part == lax.axis_size("dom") - 1, 0.0, jnp.where(odd_d, two, one))
            down = jnp.where(row_at == 0, inner, pltpu.roll(here, 1, 0))
            up = jnp.where(row_at == depth - 1, outer, pltpu.roll(here, depth - 1, 0))
            left = jnp.where(lane_at == 0, 0.0, pltpu.roll(here, 1, 1))
            right = jnp.where(lane_at == width - 1, 0.0, pltpu.roll(here, width - 1, 1))
            beside = (around[a] + around[a + 2]) + (down + up) + (left + right)
            span = slice(a * depth, (a + 1) * depth)
            factor = diag[span, :] + (6.0 - CENTRE)
            field[c, span, :] = factor * here - beside + flame[c, span, :]
    if azim_x is not None:
        write_edges(rows, depth, field, ref_part, ref_line, azim_x, azim_y, dom_x, dom_y)


def last_kernel(rows, depth, *refs):
    first, tables, powers = refs[:7], refs[7 : 7 + PARTS], refs[7 + PARTS : -4]
    dots_in, dots_out, field, held = refs[-4:]
    step_kernel(rows, depth, None, None, *first, field, None, None, None, None)
    add_dots(len(powers), None, powers, field, dots_in, dots_out, held)
    dots_out[...] += total_of(table[...] for table in tables)


def folded(x):
    tall = total_of(x[i : i + 8] for i in range(0, x.shape[0], 8))
    tile = total_of(tall[:, j : j + 128] for j in range(0, x.shape[1], 128))
    return jnp.sum(tile, axis=0, keepdims=True)


def total_of(terms):
    terms = list(terms)
    while len(terms) > 1:
        terms = [
            terms[i] + terms[i + 1] if i + 1 < len(terms) else terms[i]
            for i in range(0, len(terms), 2)
        ]
    return terms[0]


def add_dots(k, basis, powers, current, dots_in, dots_out, held):
    held[...] = jnp.zeros_like(held)
    re, im = current[0], current[1]
    count = 0
    if basis is not None:
        count = basis.shape[0]

        def one(i, carry):
            left_re, left_im = basis[i, 0], basis[i, 1]
            held[pl.ds(i, 1), :] = folded(left_re * re + left_im * im)
            held[pl.ds(count + i, 1), :] = folded(left_re * im - left_im * re)
            return carry

        lax.fori_loop(0, count, one, 0)
    first = held.shape[0] - 16
    for j, power in enumerate([*powers, current]):
        left_re, left_im = power[0], power[1]
        held[first + j : first + j + 1, :] = folded(left_re * re + left_im * im)
        held[first + 8 + j : first + 9 + j, :] = folded(left_re * im - left_im * re)
    row = lax.dot_general(
        jnp.ones((8, 128), jnp.float32), held[...], (((1,), (1,)), ((), ())),
        precision=HIGHEST, preferred_element_type=jnp.float32,
    )
    at = lax.broadcasted_iota(jnp.int32, row.shape, 0)
    wide = row.shape[1]
    dots_out[...] = jnp.zeros_like(dots_out)
    dots_out[:, :wide] = jnp.where(at == k, row, 0.0 if dots_in is None else dots_in[:, :wide])


class Cx:
    def __init__(self, re, im):
        self.re, self.im = re, im

    def __add__(self, o):
        return Cx(self.re + o.re, self.im + o.im)

    def __sub__(self, o):
        return Cx(self.re - o.re, self.im - o.im)

    def __mul__(self, o):
        if isinstance(o, Cx):
            return Cx(self.re * o.re - self.im * o.im, self.re * o.im + self.im * o.re)
        return Cx(self.re * o, self.im * o)

    def conj(self):
        return Cx(self.re, -self.im)

    def sq(self):
        return self.re * self.re + self.im * self.im


def small_problem(gram, mu):
    steps = INNER_STEPS

    def applied(vec):
        return {j: total_of(gram[j][k] * v for k, v in vec.items()) for j in range(steps + 2)}

    def dot(left, image):
        return total_of(v.conj() * image[k] for k, v in left.items())

    def less(vec, scale, other):
        out = dict(vec)
        for k, v in other.items():
            out[k] = out[k] - scale * v if k in out else Cx(-(scale * v).re, -(scale * v).im)
        return out

    def scaled(vec, by):
        return {k: v * by for k, v in vec.items()}

    def times_operator(vec, shift):
        out = {}
        for k, v in vec.items():
            out[k + 1] = v
        for k, v in vec.items():
            out[k] = out[k] + shift * v if k in out else shift * v
        return out

    first = gram[0][0].re
    unit = 1.0 / jnp.sqrt(first + EPSILON)
    zero = jnp.zeros_like(first)
    u = {0: Cx(unit, zero)}
    u_image = applied(u)
    w = times_operator(u, mu)
    w_image = applied(w)
    image_sq = dot(w, w_image).re
    cross = dot(w, u_image)
    bottom = cross.sq()
    theta = Cx(image_sq * cross.re / bottom, -image_sq * cross.im / bottom)
    r = less(w, theta, u)
    along = dot(u, applied(r))
    b = scaled(less(r, along, u), -1.0)
    beta = jnp.sqrt(dot(b, applied(b)).re + EPSILON)
    q = [scaled(b, 1.0 / beta)]
    q_image = [applied(q[0])]
    hess = []
    shift = mu - theta
    for column in range(steps):
        z = times_operator(q[-1], shift)
        z = less(z, dot(u, applied(z)), u)
        z_image = applied(z)
        column_dots = [dot(one, z_image) for one in q]
        for value, one in zip(column_dots, q):
            z = less(z, value, one)
        z_image = applied(z)
        length = jnp.sqrt(dot(z, z_image).re + EPSILON)
        hess.append((column_dots, length))
        if column + 1 < steps:
            q.append(scaled(z, 1.0 / length))
    full = []
    for column, (dots, length) in enumerate(hess):
        entries = {i: v for i, v in enumerate(dots)}
        entries[column + 1] = Cx(length, zero)
        full.append(entries)

    def column_dot(i, j):
        return total_of(full[i][k].conj() * full[j][k] for k in full[i] if k in full[j])

    low = [[None] * steps for _ in range(steps)]
    for j in range(steps):
        diagonal = column_dot(j, j).re
        for k in range(j):
            diagonal = diagonal - low[j][k].sq()
        root = jnp.sqrt(diagonal)
        low[j][j] = root
        for i in range(j + 1, steps):
            value = column_dot(i, j)
            for k in range(j):
                value = value - low[i][k] * low[j][k].conj()
            low[i][j] = value * (1.0 / root)
    middle = []
    for i in range(steps):
        value = full[i][0].conj() * beta
        for k in range(i):
            value = value - low[i][k] * middle[k]
        middle.append(value * (1.0 / low[i][i]))
    solved = [None] * steps
    for i in reversed(range(steps)):
        value = middle[i]
        for k in range(i + 1, steps):
            value = value - low[k][i].conj() * solved[k]
        solved[i] = value * (1.0 / low[i][i])
    update = {}
    for value, one in zip(solved, q):
        for k, v in one.items():
            update[k] = update[k] + value * v if k in update else value * v
    update_sq = dot(update, applied(update)).re
    return theta, update, update_sq


def end_kernel(rows, depth, scale, shift, gram_s, gram, basis, *refs):
    powers, out, ritz, column = refs[: INNER_STEPS + 1], refs[-3], refs[-2], refs[-1]
    count = basis.shape[0]
    width = basis.shape[3]
    base = 2 * count
    tile = (8, 128)

    def splat(i, j):
        return jnp.full(tile, gram_s[i, j] * scale, jnp.float32)

    size = INNER_STEPS + 2
    table = [[None] * size for _ in range(size)]
    for i in range(size):
        for j in range(i, size):
            im = splat(j, base + 8 + i) if i != j else jnp.zeros(tile, jnp.float32)
            table[i][j] = Cx(splat(j, base + i), im)
            if i != j:
                table[j][i] = table[i][j].conj()
    mu = Cx(
        jnp.full(tile, CENTRE - shift[0], jnp.float32), jnp.full(tile, -shift[1], jnp.float32)
    )
    theta, update, update_sq = small_problem(table, mu)
    ritz[0] = theta.re[0, 0]
    ritz[1] = theta.im[0, 0]

    def lanes(x):
        return jnp.sum(x, axis=1, keepdims=True)

    def sublanes(x):
        return jnp.sum(x, axis=0, keepdims=True)

    def shifted(x, by):
        return pltpu.roll(x, 128 - by, 1)

    folds = 128 // count
    table = jnp.concatenate(
        [
            shifted(gram[5 + r : 6 + r, :], count * q) if q else gram[5 + r : 6 + r, :]
            for r in range(count // folds)
            for q in range(folds)
        ],
        axis=0,
    )
    lane = lax.broadcasted_iota(jnp.int32, (count, 128), 1)
    same = lax.broadcasted_iota(jnp.int32, (count, 128), 0) == lane
    by_re = total_of(gram[k : k + 1, :] * v.re[0:1] for k, v in update.items()) * scale
    by_im = total_of(gram[k : k + 1, :] * v.im[0:1] for k, v in update.items()) * scale
    first_re = lanes(jnp.where(same, by_re - shifted(by_im, count), 0.0))
    first_im = lanes(jnp.where(same, by_im + shifted(by_re, count), 0.0))

    table = jnp.where(lane < count, table, 0.0) * (0.5 * scale)

    def across(col):
        return sublanes(jnp.where(same, col, 0.0))

    def mixed(col_re, col_im):
        def halves(col):
            straight = lanes(table * across(col))
            turned = lanes(jnp.where(same, sublanes(table * col), 0.0))
            return straight + turned, straight - turned

        re_re, im_re = halves(col_re)
        re_im, im_im = halves(col_im)
        return re_re - im_im, re_im + im_re

    mixed_re, mixed_im = mixed(first_re, first_im)
    second_re, second_im = first_re - mixed_re, first_im - mixed_im
    again_re, again_im = mixed(second_re, second_im)
    change = (
        -2.0 * (first_re * first_re + first_im * first_im)
        + (first_re * mixed_re + first_im * mixed_im)
        - 2.0 * (second_re * second_re + second_im * second_im)
        + (second_re * again_re + second_im * again_im)
    )
    final_sq = update_sq[0:1, 0:1] + sublanes(change)
    inverse = 1.0 / jnp.sqrt(final_sq + EPSILON)
    column[0] = jnp.broadcast_to((first_re + second_re) * inverse, (count, 128))
    column[1] = jnp.broadcast_to((first_im + second_im) * inverse, (count, 128))
    full_inverse = jnp.broadcast_to(inverse, tile)
    coefs = {k: v * full_inverse for k, v in update.items()}

    def wide(x):
        return jnp.tile(x[0:1, :], (1, width // 128))

    coefs = {k: Cx(wide(v.re), wide(v.im)) for k, v in coefs.items()}
    for a in range(rows):
        span = slice(a * depth, (a + 1) * depth)
        real = jnp.zeros((depth, width), jnp.float32)
        imag = real
        for k, v in coefs.items():
            re, im = powers[k][0, span, :], powers[k][1, span, :]
            real = real + (v.re * re - v.im * im)
            imag = imag + (v.re * im + v.im * re)
        for i in range(count):
            v = Cx(wide(column[0, i : i + 1, :]), wide(column[1, i : i + 1, :]))
            re, im = basis[i, 0, span, :], basis[i, 1, span, :]
            real = real - (v.re * re - v.im * im)
            imag = imag - (v.re * im + v.im * re)
        out[0, span, :] = real
        out[1, span, :] = imag


def on_device(
    search_basis, coefficients, target_shift, stiffness_diag, flame_mats,
    flame_count, flame_line, flame_burner, reference_part, reference_line,
):
    n_azim, n_dom = lax.axis_size("azim"), lax.axis_size("dom")
    count, _, rows, depth, width = search_basis.shape
    lines = rows * depth
    scale = 1.0 / float(stiffness_diag.size * n_azim * n_dom)
    slots = flame_mats.shape[0]
    base = 2 * rows
    tall = base + 2 * reference_part.shape[0]
    basis = search_basis.reshape(count, 2, lines, width)
    diag = stiffness_diag.reshape(lines, width)
    mats = flame_mats.reshape(slots, 2 * width, width)

    def exchange(values, axis, pairs):
        both = pairs + [(j, i) for i, j in pairs]
        return lax.ppermute(values, axis, both)

    azim_even = [(i, i + 1) for i in range(0, n_azim, 2)]
    azim_odd = [(i, (i + 1) % n_azim) for i in range(1, n_azim, 2)]
    dom_even = [(i, i + 1) for i in range(0, n_dom, 2)]
    dom_odd = [(i, (i + 1) % n_dom) for i in range(1, n_dom, 2)]

    def shape(*dims):
        return jax.ShapeDtypeStruct(dims, jnp.float32)

    fields = [
        shape(2, lines, width),
        shape(2, depth, width),
        shape(2, depth, width),
        shape(tall, width),
        shape(tall, width),
    ]
    power, azim_x, azim_y, dom_x, dom_y, basis = call(
        functools.partial(start_kernel, rows, depth),
        [*fields, shape(count, 2, lines, width)],
        in_hbm(4),
        held_in_hbm(coefficients, reference_part, reference_line, basis),
        [
            SMEM(coefficients.shape, jnp.float32),
            SMEM(reference_part.shape, jnp.int32),
            SMEM(reference_line.shape, jnp.int32),
            pltpu.SemaphoreType.DMA((3,)),
            pltpu.SemaphoreType.DMA((4,)),
        ],
        cost=4,
    )
    powers = [power]
    held = VMEM((2 * count + 16, 128), jnp.float32)
    tables = [
        call(
            functools.partial(basis_kernel, part, PARTS),
            shape(8, 128),
            vmem(1),
            (basis,),
            [VMEM((width // 128, count * 2 * (lines // PARTS), 128), jnp.float32)],
        )
        for part in range(PARTS)
    ]
    is_sum = lax.broadcasted_iota(jnp.int32, (tall, width), 0) >= base
    for step in range(INNER_STEPS + 1):
        from_ay = exchange(azim_y, "azim", azim_odd)
        from_dx = exchange(dom_x, "dom", dom_even)
        dom_y = jnp.where(is_sum, dom_x + from_dx, dom_y)
        from_dy = exchange(dom_y, "dom", dom_odd)
        from_ax = exchange(azim_x, "azim", azim_even)
        sums = dom_y + from_dy
        reach = 4
        while reach < n_dom:
            pairs = [(i, i ^ reach) for i in range(n_dom) if i < i ^ reach]
            sums = sums + exchange(sums, "dom", pairs)
            reach *= 2
        numbers = (flame_count, flame_line, flame_burner)
        source = VMEM((16, width), jnp.bfloat16)
        half = slots // 2
        blocks = jax.ShapeDtypeStruct((half, 2 * width, width), mats.dtype)
        if step == 0:
            (mats,) = held_in_hbm(mats)
            dots, lower = call(
                first_dots_kernel,
                [shape(8, 128), blocks],
                vmem(2) + in_hbm(1),
                (basis, power, mats),
                [held, pltpu.SemaphoreType.DMA((half,))],
                cost=2,
            )
            flame, upper = call(
                functools.partial(first_flame_kernel, base),
                [shape(2, lines, width), blocks],
                smem(3) + vmem(2) + in_hbm(1) + vmem(1),
                (*numbers, sums, lower, mats, dots),
                [source, pltpu.SemaphoreType.DMA((half,))],
                cost=3,
            )
        else:
            given = (basis, *powers, dots)
            dots = call(
                functools.partial(dots_kernel, step), shape(8, 128), vmem(len(given)), given, [held]
            )
            order = (dots, *tables[step - 1 : step])
            flame = call(
                functools.partial(flame_kernel, base),
                shape(2, lines, width),
                smem(3) + vmem(3 + len(order)),
                (*numbers, sums, lower, upper, *order),
                [source],
                cost=3,
            )
        received = (power, flame, diag, from_ax, from_ay, from_dx, from_dy)
        if step < INNER_STEPS:
            power, azim_x, azim_y, dom_x, dom_y = call(
                functools.partial(step_kernel, rows, depth),
                fields,
                smem(2) + vmem(7),
                (reference_part, reference_line, *received),
            )
        else:
            dots = call(
                functools.partial(last_kernel, rows, depth),
                shape(8, 128),
                vmem(8 + len(tables) + len(powers)),
                (*received, *tables, *powers, dots),
                [VMEM((2, lines, width), jnp.float32), held],
            )
        powers.append(power)
    devices = n_azim * n_dom
    spread = jnp.broadcast_to(dots[None], (devices, *dots.shape))
    gram = jnp.sum(lax.all_to_all(spread, ("azim", "dom"), 0, 0), axis=0)
    new_vector, ritz = call(
        functools.partial(end_kernel, rows, depth, scale),
        [shape(2, lines, width), shape(2)],
        smem(2) + vmem(2 + INNER_STEPS + 1),
        (target_shift, gram, gram, basis, *powers[: INNER_STEPS + 1]),
        [VMEM((2, count, 128), jnp.float32)],
        out_specs=[pl.BlockSpec(memory_space=VMEM), pl.BlockSpec(memory_space=SMEM)],
    )
    return new_vector.reshape(2, rows, depth, width), ritz


def solution(mesh):
    placed = (
        P(None, None, "azim", "dom", None),
        P(),
        P(),
        P("azim", "dom", None),
        P(("azim", "dom"), None, None, None),
        P(("azim", "dom")),
        P(("azim", "dom")),
        P(("azim", "dom")),
        P("azim"),
        P("azim"),
    )
    return jax.shard_map(
        on_device,
        mesh=mesh,
        in_specs=placed,
        out_specs=(P(None, "azim", "dom", None), P()),
        check_vma=False,
    )
```

```python
import functools

import jax
import jax.numpy as jnp
from jax import lax
from jax.experimental import pallas as pl
from jax.experimental.pallas import tpu as pltpu
from jax.sharding import PartitionSpec as P


INNER_STEPS = 3
EPSILON = 1e-06
CENTRE = 7.125
HIGHEST = lax.Precision.HIGHEST
VMEM = pltpu.VMEM
SMEM = pltpu.SMEM


def vmem(count):
    return [pl.BlockSpec(memory_space=VMEM) for _ in range(count)]


def smem(count):
    return [pl.BlockSpec(memory_space=SMEM) for _ in range(count)]


def in_hbm(count):
    return [pl.BlockSpec(memory_space=pltpu.HBM) for _ in range(count)]


def held_in_hbm(*arrays):
    return [pltpu.with_memory_space_constraint(a, pltpu.HBM) for a in arrays]


def call(kernel, outs, specs, args, scratch=(), cost=1, out_specs=None, aliases={}, limit=8 << 20):
    estimate = pl.CostEstimate(flops=0, transcendentals=0, bytes_accessed=cost * 2_000_000)
    if out_specs is None:
        out_specs = jax.tree.map(lambda _: pl.BlockSpec(memory_space=VMEM), outs)
    return pl.pallas_call(
        kernel,
        out_shape=outs,
        in_specs=specs,
        out_specs=out_specs,
        scratch_shapes=list(scratch),
        input_output_aliases=aliases,
        compiler_params=pltpu.CompilerParams(vmem_limit_bytes=limit),
        cost_estimate=estimate,
    )(*args)


def write_edges(rows, depth, field, ref_part, ref_line, azim_x, azim_y, dom_x, dom_y):
    odd_a = lax.axis_index("azim") % 2
    part = lax.axis_index("dom")
    odd_d = part % 2
    last = (rows - 1) * depth
    x_start = pl.multiple_of((1 - odd_a) * last, depth)
    y_start = pl.multiple_of(odd_a * last, depth)
    for c in range(2):
        azim_x[c] = field[c, pl.ds(x_start, depth), :]
        azim_y[c] = field[c, pl.ds(y_start, depth), :]
        for a in range(rows):
            x_row = a * depth + (1 - odd_d) * (depth - 1)
            y_row = a * depth + odd_d * (depth - 1)
            at = c * rows + a
            dom_x[at : at + 1, :] = field[c, pl.ds(x_row, 1), :]
            dom_y[at : at + 1, :] = field[c, pl.ds(y_row, 1), :]
    base = 2 * rows
    for b in range(ref_part.shape[0]):
        mine = ref_part[b] == part
        for c in range(2):
            at = base + 2 * b + c
            line = field[c, pl.ds(ref_line[b], 1), :]
            dom_x[at : at + 1, :] = jnp.where(mine, line, 0.0)
            dom_y[at : at + 1, :] = jnp.zeros_like(line)


def start_kernel(
    rows, depth, coef_in, part_in, line_in, basis_in,
    field, azim_x, azim_y, dom_x, dom_y, basis, coef, ref_part, ref_line, small_sems, sems,
):
    count = basis.shape[0]
    pairs = ((coef_in, coef), (part_in, ref_part), (line_in, ref_line))
    small = [pltpu.make_async_copy(a, b, small_sems.at[i]) for i, (a, b) in enumerate(pairs)]
    group = count // sems.shape[0]
    large = [
        pltpu.make_async_copy(
            basis_in.at[pl.ds(i * group, group)], basis.at[pl.ds(i * group, group)], sems.at[i]
        )
        for i in range(sems.shape[0])
    ]
    for copy in small + large:
        copy.start()
    for copy in small:
        copy.wait()
    for at, copy in enumerate(large):
        copy.wait()
        for a in range(rows):
            span = slice(a * depth, (a + 1) * depth)
            real = imag = None
            for i in range(at * group, (at + 1) * group):
                re, im = basis[i, 0, span, :], basis[i, 1, span, :]
                one = coef[0, i] * re - coef[1, i] * im
                two = coef[0, i] * im + coef[1, i] * re
                real = one if real is None else real + one
                imag = two if imag is None else imag + two
            field[0, span, :] = real if at == 0 else field[0, span, :] + real
            field[1, span, :] = imag if at == 0 else field[1, span, :] + imag
    write_edges(rows, depth, field, ref_part, ref_line, azim_x, azim_y, dom_x, dom_y)


def basis_products(part, parts, basis, tiles):
    half = basis.shape[0]
    count = 2 * half
    lines, width = basis.shape[2] // parts, basis.shape[3]
    first = part * lines
    for c in range(2):
        for i in range(half):
            for j in range(width // 128):
                at = (c * half + i) * lines
                tiles[j, at : at + lines, :] = basis[
                    i, c, first : first + lines, j * 128 : (j + 1) * 128
                ]

    def one(line):
        tall = jnp.concatenate(
            [tiles.at[j][pl.ds(line, count, stride=lines), :] for j in range(width // 128)], axis=1
        )
        high = tall.astype(jnp.bfloat16)
        low = (tall - high.astype(jnp.float32)).astype(jnp.bfloat16)
        return jnp.concatenate([high, low], axis=0)

    group = min(4, lines)

    def some(at, total):
        both = jnp.concatenate([one(at * group + i) for i in range(group)], axis=1)
        return total + lax.dot_general(
            both, both, (((1,), (1,)), ((), ())), preferred_element_type=jnp.float32
        )

    zero = jnp.zeros((2 * count, 2 * count), jnp.float32)
    total = lax.fori_loop(0, lines // group, some, zero)
    total = total[:count] + total[count:]
    total = jnp.concatenate([total, jnp.zeros((count, 128 - 2 * count), jnp.float32)], axis=1)
    total = total + pltpu.roll(total, 128 - count, 1)
    top, bottom = total[:half], total[half:]
    crossed = pltpu.roll(top, 128 - half, 1)
    lane = lax.broadcasted_iota(jnp.int32, (half, 128), 1)
    table = jnp.where(
        lane < half, top + pltpu.roll(bottom, 128 - half, 1) + crossed - bottom, 0.0
    )
    folds = 128 // half
    packed = []
    for r in range(half // folds):
        rows = [
            pltpu.roll(table[r * folds + s : r * folds + s + 1], half * s, 1) if s
            else table[r * folds : r * folds + 1]
            for s in range(folds)
        ]
        packed.append(total_of(rows))
    return packed


def add_basis_products(part, basis, tiles, dots):
    for r, row in enumerate(basis_products(part, INNER_STEPS + 1, basis, tiles)):
        dots[2 + r : 3 + r, :] += row


def dots_kernel(k, basis, *refs):
    powers, (dots_out, held, tiles) = refs[: k + 1], refs[-3:]
    add_dots(k, basis, powers[:-1], powers[-1], refs[k + 1], dots_out, held)
    add_basis_products(k, basis, tiles, dots_out)


def first_dots_kernel(
    basis, power, count, mats_in, dots_out, mats, count_out, held, tiles, sems
):
    half = sems.shape[0]
    copies = [pltpu.make_async_copy(mats_in.at[s], mats.at[s], sems.at[s]) for s in range(half)]
    for copy in copies:
        copy.start()
    add_dots(0, basis, [], power, None, dots_out, held)
    add_basis_products(0, basis, tiles, dots_out)
    count_out[...] = jnp.broadcast_to(count[...], count_out.shape)
    for copy in copies:
        copy.wait()


def flame_kernel(base, live, lines, burners, sums, mats, *refs, ready=None):
    out, source = refs[-2:]
    width = sums.shape[1]
    slots = mats.shape[0]
    half = slots // 2
    rows = sums.shape[0] - base
    source[...] = jnp.zeros_like(source)
    for i in range(rows):
        row = sums[base + i : base + i + 1, :]
        high = row.astype(jnp.bfloat16)
        source[2 * i : 2 * i + 1, :] = high
        source[2 * i + 1 : 2 * i + 2, :] = (row - high.astype(jnp.float32)).astype(jnp.bfloat16)
    out[...] = jnp.zeros_like(out)
    left = source[...]

    def products(blocks):
        return lax.dot_general(
            left, blocks, (((1,), (1,)), ((), ())), preferred_element_type=jnp.float32
        )

    def put(s, product):
        chosen = product[0:4]
        for b in range(1, rows // 2):
            chosen = jnp.where(burners[s] == b, product[4 * b : 4 * b + 4], chosen)
        by_re = chosen[0:1] + chosen[1:2]
        by_im = chosen[2:3] + chosen[3:4]
        at = pl.ds(lines[s], 1)
        out[0, at, :] += by_re[:, :width] - by_im[:, width:]
        out[1, at, :] += by_im[:, :width] + by_re[:, width:]

    def put_all(first, number):
        blocks = mats[first : first + number]
        every = products(blocks.reshape(number * 2 * width, width))
        for s in range(number):

            @pl.when(first + s < live[0, 0])
            def _():
                put(first + s, every[:, 2 * width * s : 2 * width * (s + 1)])

    few = half // 2

    @pl.when(live[0, 0] <= few)
    def _():
        def slot(s, carry):
            put(s, products(mats[s]))
            return carry

        lax.fori_loop(0, live[0, 0], slot, 0)

    if ready is None:

        @pl.when(live[0, 0] > few)
        def _():
            put_all(0, slots)
    else:

        @pl.when(live[0, 0] > few)
        def _():
            put_all(0, half)

        ready()

        @pl.when(live[0, 0] > half)
        def _():
            put_all(half, half)


def first_flame_kernel(base, live, lines, burners, sums, given, mats_in, order, out, mats, *refs):
    source, sems = refs
    half = sems.shape[0]
    copies = [
        pltpu.make_async_copy(mats_in.at[half + s], mats.at[half + s], sems.at[s])
        for s in range(half)
    ]
    for copy in copies:
        copy.start()

    def ready():
        for copy in copies:
            copy.wait()

    flame_kernel(base, live, lines, burners, sums, mats, order, out, source, ready=ready)


def step_kernel(
    rows, depth, ref_part, ref_line, old, flame, diag, from_ax, from_ay, from_dx, from_dy,
    field, azim_x, azim_y, dom_x, dom_y,
):
    width = old.shape[2]
    odd_a = lax.axis_index("azim") % 2 == 1
    part = lax.axis_index("dom")
    odd_d = part % 2 == 1
    row_at = lax.broadcasted_iota(jnp.int32, (depth, width), 0)
    lane_at = lax.broadcasted_iota(jnp.int32, (depth, width), 1)
    for c in range(2):
        before = jnp.where(odd_a, from_ax[c], from_ay[c])
        after = jnp.where(odd_a, from_ay[c], from_ax[c])
        planes = [old[c, a * depth : (a + 1) * depth, :] for a in range(rows)]
        around = [before, *planes, after]
        for a in range(rows):
            here = planes[a]
            at = c * rows + a
            one, two = from_dx[at : at + 1, :], from_dy[at : at + 1, :]
            inner = jnp.where(part == 0, 0.0, jnp.where(odd_d, one, two))
            outer = jnp.where(part == lax.axis_size("dom") - 1, 0.0, jnp.where(odd_d, two, one))
            down = jnp.where(row_at == 0, inner, pltpu.roll(here, 1, 0))
            up = jnp.where(row_at == depth - 1, outer, pltpu.roll(here, depth - 1, 0))
            left = jnp.where(lane_at == 0, 0.0, pltpu.roll(here, 1, 1))
            right = jnp.where(lane_at == width - 1, 0.0, pltpu.roll(here, width - 1, 1))
            beside = (around[a] + around[a + 2]) + (down + up) + (left + right)
            span = slice(a * depth, (a + 1) * depth)
            factor = diag[span, :] + (6.0 - CENTRE)
            field[c, span, :] = factor * here - beside + flame[c, span, :]
    if azim_x is not None:
        write_edges(rows, depth, field, ref_part, ref_line, azim_x, azim_y, dom_x, dom_y)


def last_kernel(rows, depth, *refs):
    first, powers, (dots_in, dots_out, field, held) = refs[:7], refs[7:-4], refs[-4:]
    step_kernel(rows, depth, None, None, *first, field, None, None, None, None)
    add_dots(len(powers), None, powers, field, dots_in, dots_out, held)


def folded(x):
    tall = total_of(x[i : i + 8] for i in range(0, x.shape[0], 8))
    tile = total_of(tall[:, j : j + 128] for j in range(0, x.shape[1], 128))
    return jnp.sum(tile, axis=0, keepdims=True)


def total_of(terms):
    terms = list(terms)
    while len(terms) > 1:
        terms = [
            terms[i] + terms[i + 1] if i + 1 < len(terms) else terms[i]
            for i in range(0, len(terms), 2)
        ]
    return terms[0]


def place_of(k):
    return (0, 16) if k == INNER_STEPS + 1 else (k // 2, 64 * (k % 2))


def add_dots(k, basis, powers, current, dots_in, dots_out, held):
    held[...] = jnp.zeros_like(held)
    re, im = current[0], current[1]
    count = 0
    if basis is not None:
        count = basis.shape[0]

        def one(i, carry):
            left_re, left_im = basis[i, 0], basis[i, 1]
            held[pl.ds(i, 1), :] = folded(left_re * re + left_im * im)
            held[pl.ds(count + i, 1), :] = folded(left_re * im - left_im * re)
            return carry

        lax.fori_loop(0, count, one, 0)
    first = held.shape[0] - 16
    for j, power in enumerate([*powers, current]):
        left_re, left_im = power[0], power[1]
        held[first + j : first + j + 1, :] = folded(left_re * re + left_im * im)
        held[first + 8 + j : first + 9 + j, :] = folded(left_re * im - left_im * re)
    row = lax.dot_general(
        jnp.ones((8, 128), jnp.float32), held[...], (((1,), (1,)), ((), ())),
        precision=HIGHEST, preferred_element_type=jnp.float32,
    )
    row = jnp.concatenate([row, jnp.zeros((8, 128 - row.shape[1]), jnp.float32)], axis=1)
    at, lane = place_of(k)
    row = pltpu.roll(row, lane, 1) if lane else row
    dots_out[...] = jnp.zeros_like(dots_out) if dots_in is None else dots_in[...]
    dots_out[at : at + 1, :] += row[0:1]


class Cx:
    def __init__(self, re, im):
        self.re, self.im = re, im

    def __add__(self, o):
        return Cx(self.re + o.re, self.im + o.im)

    def __sub__(self, o):
        return Cx(self.re - o.re, self.im - o.im)

    def __mul__(self, o):
        if isinstance(o, Cx):
            return Cx(self.re * o.re - self.im * o.im, self.re * o.im + self.im * o.re)
        return Cx(self.re * o, self.im * o)

    def conj(self):
        return Cx(self.re, -self.im)

    def sq(self):
        return self.re * self.re + self.im * self.im


def small_problem(gram, mu):
    steps = INNER_STEPS

    def applied(vec):
        return {j: total_of(gram[j][k] * v for k, v in vec.items()) for j in range(steps + 2)}

    def dot(left, image):
        return total_of(v.conj() * image[k] for k, v in left.items())

    def less(vec, scale, other):
        out = dict(vec)
        for k, v in other.items():
            out[k] = out[k] - scale * v if k in out else Cx(-(scale * v).re, -(scale * v).im)
        return out

    def scaled(vec, by):
        return {k: v * by for k, v in vec.items()}

    def times_operator(vec, shift):
        out = {}
        for k, v in vec.items():
            out[k + 1] = v
        for k, v in vec.items():
            out[k] = out[k] + shift * v if k in out else shift * v
        return out

    first = gram[0][0].re
    unit = 1.0 / jnp.sqrt(first + EPSILON)
    zero = jnp.zeros_like(first)
    u = {0: Cx(unit, zero)}
    u_image = applied(u)
    w = times_operator(u, mu)
    w_image = applied(w)
    image_sq = dot(w, w_image).re
    cross = dot(w, u_image)
    bottom = cross.sq()
    theta = Cx(image_sq * cross.re / bottom, -image_sq * cross.im / bottom)
    r = less(w, theta, u)
    along = dot(u, applied(r))
    b = scaled(less(r, along, u), -1.0)
    beta = jnp.sqrt(dot(b, applied(b)).re + EPSILON)
    q = [scaled(b, 1.0 / beta)]
    q_image = [applied(q[0])]
    hess = []
    shift = mu - theta
    for column in range(steps):
        z = times_operator(q[-1], shift)
        z = less(z, dot(u, applied(z)), u)
        z_image = applied(z)
        column_dots = [dot(one, z_image) for one in q]
        for value, one in zip(column_dots, q):
            z = less(z, value, one)
        z_image = applied(z)
        length = jnp.sqrt(dot(z, z_image).re + EPSILON)
        hess.append((column_dots, length))
        if column + 1 < steps:
            q.append(scaled(z, 1.0 / length))
    full = []
    for column, (dots, length) in enumerate(hess):
        entries = {i: v for i, v in enumerate(dots)}
        entries[column + 1] = Cx(length, zero)
        full.append(entries)

    def column_dot(i, j):
        return total_of(full[i][k].conj() * full[j][k] for k in full[i] if k in full[j])

    low = [[None] * steps for _ in range(steps)]
    for j in range(steps):
        diagonal = column_dot(j, j).re
        for k in range(j):
            diagonal = diagonal - low[j][k].sq()
        root = jnp.sqrt(diagonal)
        low[j][j] = root
        for i in range(j + 1, steps):
            value = column_dot(i, j)
            for k in range(j):
                value = value - low[i][k] * low[j][k].conj()
            low[i][j] = value * (1.0 / root)
    middle = []
    for i in range(steps):
        value = full[i][0].conj() * beta
        for k in range(i):
            value = value - low[i][k] * middle[k]
        middle.append(value * (1.0 / low[i][i]))
    solved = [None] * steps
    for i in reversed(range(steps)):
        value = middle[i]
        for k in range(i + 1, steps):
            value = value - low[k][i].conj() * solved[k]
        solved[i] = value * (1.0 / low[i][i])
    update = {}
    for value, one in zip(solved, q):
        for k, v in one.items():
            update[k] = update[k] + value * v if k in update else value * v
    update_sq = dot(update, applied(update)).re
    return theta, update, update_sq


def end_kernel(rows, depth, scale, shift, gram_s, gram, basis, *refs):
    powers, out, ritz, column = refs[: INNER_STEPS + 1], refs[-3], refs[-2], refs[-1]
    count = basis.shape[0]
    width = basis.shape[3]
    base = 2 * count
    tile = (8, 128)

    def splat(i, j):
        return jnp.full(tile, gram_s[i, j] * scale, jnp.float32)

    size = INNER_STEPS + 2
    table = [[None] * size for _ in range(size)]
    for i in range(size):
        for j in range(i, size):
            at, first = place_of(j)
            first += base + i
            im = splat(at, first + 8) if i != j else jnp.zeros(tile, jnp.float32)
            table[i][j] = Cx(splat(at, first), im)
            if i != j:
                table[j][i] = table[i][j].conj()
    mu = Cx(
        jnp.full(tile, CENTRE - shift[0], jnp.float32), jnp.full(tile, -shift[1], jnp.float32)
    )
    theta, update, update_sq = small_problem(table, mu)
    ritz[0] = theta.re[0, 0]
    ritz[1] = theta.im[0, 0]

    def lanes(x):
        return jnp.sum(x, axis=1, keepdims=True)

    def sublanes(x):
        return jnp.sum(x, axis=0, keepdims=True)

    def shifted(x, by):
        return pltpu.roll(x, 128 - by, 1)

    folds = 128 // count
    table = jnp.concatenate(
        [
            shifted(gram[2 + r : 3 + r, :], count * q) if q else gram[2 + r : 3 + r, :]
            for r in range(count // folds)
            for q in range(folds)
        ],
        axis=0,
    )
    lane = lax.broadcasted_iota(jnp.int32, (count, 128), 1)
    same = lax.broadcasted_iota(jnp.int32, (count, 128), 0) == lane

    def of_power(k):
        at, first = place_of(k)
        return shifted(gram[at : at + 1, :], first) if first else gram[at : at + 1, :]

    by_re = total_of(of_power(k) * v.re[0:1] for k, v in update.items()) * scale
    by_im = total_of(of_power(k) * v.im[0:1] for k, v in update.items()) * scale
    first_re = lanes(jnp.where(same, by_re - shifted(by_im, count), 0.0))
    first_im = lanes(jnp.where(same, by_im + shifted(by_re, count), 0.0))

    table = jnp.where(lane < count, table, 0.0) * (0.5 * scale)

    def across(col):
        return sublanes(jnp.where(same, col, 0.0))

    def mixed(col_re, col_im):
        def halves(col):
            straight = lanes(table * across(col))
            turned = lanes(jnp.where(same, sublanes(table * col), 0.0))
            return straight + turned, straight - turned

        re_re, im_re = halves(col_re)
        re_im, im_im = halves(col_im)
        return re_re - im_im, re_im + im_re

    mixed_re, mixed_im = mixed(first_re, first_im)
    second_re, second_im = first_re - mixed_re, first_im - mixed_im
    again_re, again_im = mixed(second_re, second_im)
    change = (
        -2.0 * (first_re * first_re + first_im * first_im)
        + (first_re * mixed_re + first_im * mixed_im)
        - 2.0 * (second_re * second_re + second_im * second_im)
        + (second_re * again_re + second_im * again_im)
    )
    final_sq = update_sq[0:1, 0:1] + sublanes(change)
    inverse = 1.0 / jnp.sqrt(final_sq + EPSILON)
    column[0] = jnp.broadcast_to((first_re + second_re) * inverse, (count, 128))
    column[1] = jnp.broadcast_to((first_im + second_im) * inverse, (count, 128))
    full_inverse = jnp.broadcast_to(inverse, tile)
    coefs = {k: v * full_inverse for k, v in update.items()}

    def wide(x):
        return jnp.tile(x[0:1, :], (1, width // 128))

    coefs = {k: Cx(wide(v.re), wide(v.im)) for k, v in coefs.items()}
    for a in range(rows):
        span = slice(a * depth, (a + 1) * depth)
        real = jnp.zeros((depth, width), jnp.float32)
        imag = real
        for k, v in coefs.items():
            re, im = powers[k][0, span, :], powers[k][1, span, :]
            real = real + (v.re * re - v.im * im)
            imag = imag + (v.re * im + v.im * re)
        for i in range(count):
            v = Cx(wide(column[0, i : i + 1, :]), wide(column[1, i : i + 1, :]))
            re, im = basis[i, 0, span, :], basis[i, 1, span, :]
            real = real - (v.re * re - v.im * im)
            imag = imag - (v.re * im + v.im * re)
        out[0, span, :] = real
        out[1, span, :] = imag


def on_device(
    search_basis, coefficients, target_shift, stiffness_diag, flame_mats,
    flame_count, flame_line, flame_burner, reference_part, reference_line,
):
    n_azim, n_dom = lax.axis_size("azim"), lax.axis_size("dom")
    count, _, rows, depth, width = search_basis.shape
    lines = rows * depth
    scale = 1.0 / float(stiffness_diag.size * n_azim * n_dom)
    slots = flame_mats.shape[0]
    base = 2 * rows
    tall = base + 2 * reference_part.shape[0]
    basis = search_basis.reshape(count, 2, lines, width)
    diag = stiffness_diag.reshape(lines, width)
    mats = flame_mats.reshape(slots, 2 * width, width)

    def exchange(values, axis, pairs):
        both = pairs + [(j, i) for i, j in pairs]
        return lax.ppermute(values, axis, both)

    azim_even = [(i, i + 1) for i in range(0, n_azim, 2)]
    azim_odd = [(i, (i + 1) % n_azim) for i in range(1, n_azim, 2)]
    dom_even = [(i, i + 1) for i in range(0, n_dom, 2)]
    dom_odd = [(i, (i + 1) % n_dom) for i in range(1, n_dom, 2)]

    def shape(*dims):
        return jax.ShapeDtypeStruct(dims, jnp.float32)

    fields = [
        shape(2, lines, width),
        shape(2, depth, width),
        shape(2, depth, width),
        shape(tall, width),
        shape(tall, width),
    ]
    power, azim_x, azim_y, dom_x, dom_y, basis = call(
        functools.partial(start_kernel, rows, depth),
        [*fields, shape(count, 2, lines, width)],
        in_hbm(4),
        held_in_hbm(coefficients, reference_part, reference_line, basis),
        [
            SMEM(coefficients.shape, jnp.float32),
            SMEM(reference_part.shape, jnp.int32),
            SMEM(reference_line.shape, jnp.int32),
            pltpu.SemaphoreType.DMA((3,)),
            pltpu.SemaphoreType.DMA((4,)),
        ],
        cost=4,
    )
    powers = [power]
    held = VMEM((2 * count + 16, 128), jnp.float32)
    tiles = VMEM((width // 128, count * 2 * (lines // (INNER_STEPS + 1)), 128), jnp.float32)
    is_sum = lax.broadcasted_iota(jnp.int32, (tall, width), 0) >= base
    for step in range(INNER_STEPS + 1):
        from_dx = exchange(dom_x, "dom", dom_even)
        from_ax = exchange(azim_x, "azim", azim_even)
        from_ay = exchange(azim_y, "azim", azim_odd)
        dom_y = jnp.where(is_sum, dom_x + from_dx, dom_y)
        from_dy = exchange(dom_y, "dom", dom_odd)
        sums = dom_y + from_dy
        reach = 4
        while reach < n_dom:
            pairs = [(i, i ^ reach) for i in range(n_dom) if i < i ^ reach]
            sums = sums + exchange(sums, "dom", pairs)
            reach *= 2
        half = slots // 2
        blocks = jax.ShapeDtypeStruct(mats.shape, mats.dtype)
        source = VMEM((16, width), jnp.bfloat16)
        if step == 0:
            (mats_in,) = held_in_hbm(mats)
            dots, mats, live = call(
                first_dots_kernel,
                [shape(4, 128), blocks, jax.ShapeDtypeStruct((8, 128), jnp.int32)],
                vmem(3) + in_hbm(1),
                (basis, power, flame_count.reshape(1, 1), mats_in),
                [held, tiles, pltpu.SemaphoreType.DMA((half,))],
                cost=2,
            )
        else:
            given = (basis, *powers, dots)
            dots = call(
                functools.partial(dots_kernel, step),
                shape(4, 128),
                vmem(len(given)),
                given,
                [held, tiles],
            )
        numbers = (live, flame_line, flame_burner)
        if step == 0:
            flame, mats = call(
                functools.partial(first_flame_kernel, base),
                [shape(2, lines, width), blocks],
                smem(3) + vmem(2) + in_hbm(1) + vmem(1),
                (*numbers, sums, mats, mats_in, dots),
                [source, pltpu.SemaphoreType.DMA((half,))],
                cost=3,
                aliases={4: 1},
            )
        else:
            flame = call(
                functools.partial(flame_kernel, base),
                shape(2, lines, width),
                smem(3) + vmem(3),
                (*numbers, sums, mats, dots),
                [source],
                cost=3,
            )
        received = (power, flame, diag, from_ax, from_ay, from_dx, from_dy)
        if step < INNER_STEPS:
            power, azim_x, azim_y, dom_x, dom_y = call(
                functools.partial(step_kernel, rows, depth),
                fields,
                smem(2) + vmem(7),
                (reference_part, reference_line, *received),
            )
        else:
            dots = call(
                functools.partial(last_kernel, rows, depth),
                shape(4, 128),
                vmem(8 + len(powers)),
                (*received, *powers, dots),
                [VMEM((2, lines, width), jnp.float32), held],
            )
        powers.append(power)
    devices = n_azim * n_dom
    spread = jnp.broadcast_to(dots[None], (devices, *dots.shape))
    gram = jnp.sum(lax.all_to_all(spread, ("azim", "dom"), 0, 0), axis=0)
    new_vector, ritz = call(
        functools.partial(end_kernel, rows, depth, scale),
        [shape(2, lines, width), shape(2)],
        smem(2) + vmem(2 + INNER_STEPS + 1),
        (target_shift, gram, gram, basis, *powers[: INNER_STEPS + 1]),
        [VMEM((2, count, 128), jnp.float32)],
        out_specs=[pl.BlockSpec(memory_space=VMEM), pl.BlockSpec(memory_space=SMEM)],
    )
    return new_vector.reshape(2, rows, depth, width), ritz


def solution(mesh):
    placed = (
        P(None, None, "azim", "dom", None),
        P(),
        P(),
        P("azim", "dom", None),
        P(("azim", "dom"), None, None, None),
        P(("azim", "dom")),
        P(("azim", "dom")),
        P(("azim", "dom")),
        P("azim"),
        P("azim"),
    )
    return jax.shard_map(
        on_device,
        mesh=mesh,
        in_specs=placed,
        out_specs=(P(None, "azim", "dom", None), P()),
        check_vma=False,
    )
```

```python
import functools

import jax
import jax.numpy as jnp
from jax import lax
from jax.experimental import pallas as pl
from jax.experimental.pallas import tpu as pltpu
from jax.sharding import PartitionSpec as P


INNER_STEPS = 3
EPSILON = 1e-06
CENTRE = 7.125
HIGHEST = lax.Precision.HIGHEST
VMEM = pltpu.VMEM
SMEM = pltpu.SMEM


def vmem(count):
    return [pl.BlockSpec(memory_space=VMEM) for _ in range(count)]


def smem(count):
    return [pl.BlockSpec(memory_space=SMEM) for _ in range(count)]


def in_hbm(count):
    return [pl.BlockSpec(memory_space=pltpu.HBM) for _ in range(count)]


def held_in_hbm(*arrays):
    return [pltpu.with_memory_space_constraint(a, pltpu.HBM) for a in arrays]


def call(kernel, outs, specs, args, scratch=(), cost=1, out_specs=None, aliases={}, limit=8 << 20):
    estimate = pl.CostEstimate(flops=0, transcendentals=0, bytes_accessed=cost * 2_000_000)
    if out_specs is None:
        out_specs = jax.tree.map(lambda _: pl.BlockSpec(memory_space=VMEM), outs)
    return pl.pallas_call(
        kernel,
        out_shape=outs,
        in_specs=specs,
        out_specs=out_specs,
        scratch_shapes=list(scratch),
        input_output_aliases=aliases,
        compiler_params=pltpu.CompilerParams(vmem_limit_bytes=limit),
        cost_estimate=estimate,
    )(*args)


def write_edges(rows, depth, field, ref_part, ref_line, azim_x, azim_y, dom_x, dom_y):
    odd_a = lax.axis_index("azim") % 2
    part = lax.axis_index("dom")
    odd_d = part % 2
    last = (rows - 1) * depth
    x_start = pl.multiple_of((1 - odd_a) * last, depth)
    y_start = pl.multiple_of(odd_a * last, depth)
    for c in range(2):
        azim_x[c] = field[c, pl.ds(x_start, depth), :]
        azim_y[c] = field[c, pl.ds(y_start, depth), :]
        for a in range(rows):
            x_row = a * depth + (1 - odd_d) * (depth - 1)
            y_row = a * depth + odd_d * (depth - 1)
            at = c * rows + a
            dom_x[at : at + 1, :] = field[c, pl.ds(x_row, 1), :]
            dom_y[at : at + 1, :] = field[c, pl.ds(y_row, 1), :]
    base = 2 * rows
    for b in range(ref_part.shape[0]):
        mine = ref_part[b] == part
        for c in range(2):
            at = base + 2 * b + c
            line = field[c, pl.ds(ref_line[b], 1), :]
            dom_x[at : at + 1, :] = jnp.where(mine, line, 0.0)
            dom_y[at : at + 1, :] = jnp.zeros_like(line)


def bring(source, target, first, sems):
    return [
        pltpu.make_async_copy(source.at[first + s], target.at[first + s], sems.at[s])
        for s in range(sems.shape[0])
    ]


def start_kernel(
    rows, depth, coef_in, part_in, line_in, basis_in, mats_in,
    field, azim_x, azim_y, dom_x, dom_y, basis, mats,
    coef, ref_part, ref_line, small_sems, sems, block_sems,
):
    count = basis.shape[0]
    pairs = ((coef_in, coef), (part_in, ref_part), (line_in, ref_line))
    small = [pltpu.make_async_copy(a, b, small_sems.at[i]) for i, (a, b) in enumerate(pairs)]
    group = count // sems.shape[0]
    large = [
        pltpu.make_async_copy(
            basis_in.at[pl.ds(i * group, group)], basis.at[pl.ds(i * group, group)], sems.at[i]
        )
        for i in range(sems.shape[0])
    ]
    blocks = bring(mats_in, mats, 0, block_sems)
    for copy in small + large + blocks:
        copy.start()
    for copy in small:
        copy.wait()
    for at, copy in enumerate(large):
        copy.wait()
        for a in range(rows):
            span = slice(a * depth, (a + 1) * depth)
            real = imag = None
            for i in range(at * group, (at + 1) * group):
                re, im = basis[i, 0, span, :], basis[i, 1, span, :]
                one = coef[0, i] * re - coef[1, i] * im
                two = coef[0, i] * im + coef[1, i] * re
                real = one if real is None else real + one
                imag = two if imag is None else imag + two
            field[0, span, :] = real if at == 0 else field[0, span, :] + real
            field[1, span, :] = imag if at == 0 else field[1, span, :] + imag
    write_edges(rows, depth, field, ref_part, ref_line, azim_x, azim_y, dom_x, dom_y)
    for copy in blocks:
        copy.wait()


def basis_products(part, parts, basis, tiles):
    half = basis.shape[0]
    count = 2 * half
    lines, width = basis.shape[2] // parts, basis.shape[3]
    first = part * lines
    for c in range(2):
        for i in range(half):
            for j in range(width // 128):
                at = (c * half + i) * lines
                tiles[j, at : at + lines, :] = basis[
                    i, c, first : first + lines, j * 128 : (j + 1) * 128
                ]

    def one(line):
        tall = jnp.concatenate(
            [tiles.at[j][pl.ds(line, count, stride=lines), :] for j in range(width // 128)], axis=1
        )
        high = tall.astype(jnp.bfloat16)
        low = (tall - high.astype(jnp.float32)).astype(jnp.bfloat16)
        return jnp.concatenate([high, low], axis=0)

    group = min(4, lines)

    def some(at, total):
        both = jnp.concatenate([one(at * group + i) for i in range(group)], axis=1)
        return total + lax.dot_general(
            both, both, (((1,), (1,)), ((), ())), preferred_element_type=jnp.float32
        )

    zero = jnp.zeros((2 * count, 2 * count), jnp.float32)
    total = lax.fori_loop(0, lines // group, some, zero)
    total = total[:count] + total[count:]
    total = jnp.concatenate([total, jnp.zeros((count, 128 - 2 * count), jnp.float32)], axis=1)
    total = total + pltpu.roll(total, 128 - count, 1)
    top, bottom = total[:half], total[half:]
    crossed = pltpu.roll(top, 128 - half, 1)
    lane = lax.broadcasted_iota(jnp.int32, (half, 128), 1)
    table = jnp.where(
        lane < half, top + pltpu.roll(bottom, 128 - half, 1) + crossed - bottom, 0.0
    )
    folds = 128 // half
    packed = []
    for r in range(half // folds):
        rows = [
            pltpu.roll(table[r * folds + s : r * folds + s + 1], half * s, 1) if s
            else table[r * folds : r * folds + 1]
            for s in range(folds)
        ]
        packed.append(total_of(rows))
    return packed


def add_basis_products(part, basis, tiles, dots):
    for r, row in enumerate(basis_products(part, INNER_STEPS + 1, basis, tiles)):
        dots[2 + r : 3 + r, :] += row


def dots_kernel(k, basis, *refs):
    powers, (dots_out, held, tiles) = refs[: k + 1], refs[-3:]
    add_dots(k, basis, powers[:-1], powers[-1], refs[k + 1], dots_out, held)
    add_basis_products(k, basis, tiles, dots_out)


def first_dots_kernel(
    first, basis, power, count, given, mats_in, dots_out, mats, count_out, held, tiles, sems
):
    copies = bring(mats_in, mats, first, sems)
    for copy in copies:
        copy.start()
    add_dots(0, basis, [], power, None, dots_out, held)
    add_basis_products(0, basis, tiles, dots_out)
    count_out[...] = jnp.broadcast_to(count[...], count_out.shape)
    for copy in copies:
        copy.wait()


def flame_kernel(base, live, lines, burners, sums, mats, *refs, ready=None):
    out, source = refs[-2:]
    width = sums.shape[1]
    slots = mats.shape[0]
    rows = sums.shape[0] - base
    source[...] = jnp.zeros_like(source)
    for i in range(rows):
        row = sums[base + i : base + i + 1, :]
        high = row.astype(jnp.bfloat16)
        source[2 * i : 2 * i + 1, :] = high
        source[2 * i + 1 : 2 * i + 2, :] = (row - high.astype(jnp.float32)).astype(jnp.bfloat16)
    out[...] = jnp.zeros_like(out)
    left = source[...]

    def products(blocks):
        return lax.dot_general(
            left, blocks, (((1,), (1,)), ((), ())), preferred_element_type=jnp.float32
        )

    def put(s, product):
        chosen = product[0:4]
        for b in range(1, rows // 2):
            chosen = jnp.where(burners[s] == b, product[4 * b : 4 * b + 4], chosen)
        by_re = chosen[0:1] + chosen[1:2]
        by_im = chosen[2:3] + chosen[3:4]
        at = pl.ds(lines[s], 1)
        out[0, at, :] += by_re[:, :width] - by_im[:, width:]
        out[1, at, :] += by_im[:, :width] + by_re[:, width:]

    def put_all(first, number):
        blocks = mats[first : first + number]
        every = products(blocks.reshape(number * 2 * width, width))
        for s in range(number):

            @pl.when(first + s < live[0, 0])
            def _():
                put(first + s, every[:, 2 * width * s : 2 * width * (s + 1)])

    few = 2

    @pl.when(live[0, 0] <= few)
    def _():
        def slot(s, carry):
            put(s, products(mats[s]))
            return carry

        lax.fori_loop(0, live[0, 0], slot, 0)

    if ready is None:

        @pl.when(live[0, 0] > few)
        def _():
            put_all(0, slots)
    else:
        there, wait = ready

        @pl.when(live[0, 0] > few)
        def _():
            put_all(0, there)

        wait()

        @pl.when(live[0, 0] > there)
        def _():
            put_all(there, slots - there)


def first_flame_kernel(
    base, first, live, lines, burners, sums, given, mats_in, order, out, mats, source, sems
):
    copies = bring(mats_in, mats, first, sems)
    for copy in copies:
        copy.start()

    def ready():
        for copy in copies:
            copy.wait()

    flame_kernel(base, live, lines, burners, sums, mats, order, out, source, ready=(first, ready))


def step_kernel(
    rows, depth, ref_part, ref_line, old, flame, diag, from_ax, from_ay, from_dx, from_dy,
    field, azim_x, azim_y, dom_x, dom_y,
):
    width = old.shape[2]
    odd_a = lax.axis_index("azim") % 2 == 1
    part = lax.axis_index("dom")
    odd_d = part % 2 == 1
    row_at = lax.broadcasted_iota(jnp.int32, (depth, width), 0)
    lane_at = lax.broadcasted_iota(jnp.int32, (depth, width), 1)
    for c in range(2):
        before = jnp.where(odd_a, from_ax[c], from_ay[c])
        after = jnp.where(odd_a, from_ay[c], from_ax[c])
        planes = [old[c, a * depth : (a + 1) * depth, :] for a in range(rows)]
        around = [before, *planes, after]
        for a in range(rows):
            here = planes[a]
            at = c * rows + a
            one, two = from_dx[at : at + 1, :], from_dy[at : at + 1, :]
            inner = jnp.where(part == 0, 0.0, jnp.where(odd_d, one, two))
            outer = jnp.where(part == lax.axis_size("dom") - 1, 0.0, jnp.where(odd_d, two, one))
            down = jnp.where(row_at == 0, inner, pltpu.roll(here, 1, 0))
            up = jnp.where(row_at == depth - 1, outer, pltpu.roll(here, depth - 1, 0))
            left = jnp.where(lane_at == 0, 0.0, pltpu.roll(here, 1, 1))
            right = jnp.where(lane_at == width - 1, 0.0, pltpu.roll(here, width - 1, 1))
            beside = (around[a] + around[a + 2]) + (down + up) + (left + right)
            span = slice(a * depth, (a + 1) * depth)
            factor = diag[span, :] + (6.0 - CENTRE)
            field[c, span, :] = factor * here - beside + flame[c, span, :]
    if azim_x is not None:
        write_edges(rows, depth, field, ref_part, ref_line, azim_x, azim_y, dom_x, dom_y)


def last_kernel(rows, depth, *refs):
    first, powers, (dots_in, dots_out, field, held) = refs[:7], refs[7:-4], refs[-4:]
    step_kernel(rows, depth, None, None, *first, field, None, None, None, None)
    add_dots(len(powers), None, powers, field, dots_in, dots_out, held)


def folded(x):
    tall = total_of(x[i : i + 8] for i in range(0, x.shape[0], 8))
    tile = total_of(tall[:, j : j + 128] for j in range(0, x.shape[1], 128))
    return jnp.sum(tile, axis=0, keepdims=True)


def total_of(terms):
    terms = list(terms)
    while len(terms) > 1:
        terms = [
            terms[i] + terms[i + 1] if i + 1 < len(terms) else terms[i]
            for i in range(0, len(terms), 2)
        ]
    return terms[0]


def place_of(k):
    return (0, 16) if k == INNER_STEPS + 1 else (k // 2, 64 * (k % 2))


def add_dots(k, basis, powers, current, dots_in, dots_out, held):
    held[...] = jnp.zeros_like(held)
    re, im = current[0], current[1]
    count = 0
    if basis is not None:
        count = basis.shape[0]

        def one(i, carry):
            left_re, left_im = basis[i, 0], basis[i, 1]
            held[pl.ds(i, 1), :] = folded(left_re * re + left_im * im)
            held[pl.ds(count + i, 1), :] = folded(left_re * im - left_im * re)
            return carry

        lax.fori_loop(0, count, one, 0)
    first = held.shape[0] - 16
    for j, power in enumerate([*powers, current]):
        left_re, left_im = power[0], power[1]
        held[first + j : first + j + 1, :] = folded(left_re * re + left_im * im)
        held[first + 8 + j : first + 9 + j, :] = folded(left_re * im - left_im * re)
    row = lax.dot_general(
        jnp.ones((8, 128), jnp.float32), held[...], (((1,), (1,)), ((), ())),
        precision=HIGHEST, preferred_element_type=jnp.float32,
    )
    row = jnp.concatenate([row, jnp.zeros((8, 128 - row.shape[1]), jnp.float32)], axis=1)
    at, lane = place_of(k)
    row = pltpu.roll(row, lane, 1) if lane else row
    dots_out[...] = jnp.zeros_like(dots_out) if dots_in is None else dots_in[...]
    dots_out[at : at + 1, :] += row[0:1]


class Cx:
    def __init__(self, re, im):
        self.re, self.im = re, im

    def __add__(self, o):
        return Cx(self.re + o.re, self.im + o.im)

    def __sub__(self, o):
        return Cx(self.re - o.re, self.im - o.im)

    def __mul__(self, o):
        if isinstance(o, Cx):
            return Cx(self.re * o.re - self.im * o.im, self.re * o.im + self.im * o.re)
        return Cx(self.re * o, self.im * o)

    def conj(self):
        return Cx(self.re, -self.im)

    def sq(self):
        return self.re * self.re + self.im * self.im


def small_problem(gram, mu):
    steps = INNER_STEPS

    def applied(vec):
        return {j: total_of(gram[j][k] * v for k, v in vec.items()) for j in range(steps + 2)}

    def dot(left, image):
        return total_of(v.conj() * image[k] for k, v in left.items())

    def less(vec, scale, other):
        out = dict(vec)
        for k, v in other.items():
            out[k] = out[k] - scale * v if k in out else Cx(-(scale * v).re, -(scale * v).im)
        return out

    def scaled(vec, by):
        return {k: v * by for k, v in vec.items()}

    def times_operator(vec, shift):
        out = {}
        for k, v in vec.items():
            out[k + 1] = v
        for k, v in vec.items():
            out[k] = out[k] + shift * v if k in out else shift * v
        return out

    first = gram[0][0].re
    unit = 1.0 / jnp.sqrt(first + EPSILON)
    zero = jnp.zeros_like(first)
    u = {0: Cx(unit, zero)}
    u_image = applied(u)
    w = times_operator(u, mu)
    w_image = applied(w)
    image_sq = dot(w, w_image).re
    cross = dot(w, u_image)
    bottom = cross.sq()
    theta = Cx(image_sq * cross.re / bottom, -image_sq * cross.im / bottom)
    r = less(w, theta, u)
    along = dot(u, applied(r))
    b = scaled(less(r, along, u), -1.0)
    beta = jnp.sqrt(dot(b, applied(b)).re + EPSILON)
    q = [scaled(b, 1.0 / beta)]
    q_image = [applied(q[0])]
    hess = []
    shift = mu - theta
    for column in range(steps):
        z = times_operator(q[-1], shift)
        z = less(z, dot(u, applied(z)), u)
        z_image = applied(z)
        column_dots = [dot(one, z_image) for one in q]
        for value, one in zip(column_dots, q):
            z = less(z, value, one)
        z_image = applied(z)
        length = jnp.sqrt(dot(z, z_image).re + EPSILON)
        hess.append((column_dots, length))
        if column + 1 < steps:
            q.append(scaled(z, 1.0 / length))
    full = []
    for column, (dots, length) in enumerate(hess):
        entries = {i: v for i, v in enumerate(dots)}
        entries[column + 1] = Cx(length, zero)
        full.append(entries)

    def column_dot(i, j):
        return total_of(full[i][k].conj() * full[j][k] for k in full[i] if k in full[j])

    low = [[None] * steps for _ in range(steps)]
    for j in range(steps):
        diagonal = column_dot(j, j).re
        for k in range(j):
            diagonal = diagonal - low[j][k].sq()
        root = jnp.sqrt(diagonal)
        low[j][j] = root
        for i in range(j + 1, steps):
            value = column_dot(i, j)
            for k in range(j):
                value = value - low[i][k] * low[j][k].conj()
            low[i][j] = value * (1.0 / root)
    middle = []
    for i in range(steps):
        value = full[i][0].conj() * beta
        for k in range(i):
            value = value - low[i][k] * middle[k]
        middle.append(value * (1.0 / low[i][i]))
    solved = [None] * steps
    for i in reversed(range(steps)):
        value = middle[i]
        for k in range(i + 1, steps):
            value = value - low[k][i].conj() * solved[k]
        solved[i] = value * (1.0 / low[i][i])
    update = {}
    for value, one in zip(solved, q):
        for k, v in one.items():
            update[k] = update[k] + value * v if k in update else value * v
    update_sq = dot(update, applied(update)).re
    return theta, update, update_sq


def end_kernel(rows, depth, scale, shift, gram_s, gram, basis, *refs):
    powers, out, ritz, column = refs[: INNER_STEPS + 1], refs[-3], refs[-2], refs[-1]
    count = basis.shape[0]
    width = basis.shape[3]
    base = 2 * count
    tile = (8, 128)

    def splat(i, j):
        return jnp.full(tile, gram_s[i, j] * scale, jnp.float32)

    size = INNER_STEPS + 2
    table = [[None] * size for _ in range(size)]
    for i in range(size):
        for j in range(i, size):
            at, first = place_of(j)
            first += base + i
            im = splat(at, first + 8) if i != j else jnp.zeros(tile, jnp.float32)
            table[i][j] = Cx(splat(at, first), im)
            if i != j:
                table[j][i] = table[i][j].conj()
    mu = Cx(
        jnp.full(tile, CENTRE - shift[0], jnp.float32), jnp.full(tile, -shift[1], jnp.float32)
    )
    theta, update, update_sq = small_problem(table, mu)
    ritz[0] = theta.re[0, 0]
    ritz[1] = theta.im[0, 0]

    def lanes(x):
        return jnp.sum(x, axis=1, keepdims=True)

    def sublanes(x):
        return jnp.sum(x, axis=0, keepdims=True)

    def shifted(x, by):
        return pltpu.roll(x, 128 - by, 1)

    folds = 128 // count
    table = jnp.concatenate(
        [
            shifted(gram[2 + r : 3 + r, :], count * q) if q else gram[2 + r : 3 + r, :]
            for r in range(count // folds)
            for q in range(folds)
        ],
        axis=0,
    )
    lane = lax.broadcasted_iota(jnp.int32, (count, 128), 1)
    same = lax.broadcasted_iota(jnp.int32, (count, 128), 0) == lane

    def of_power(k):
        at, first = place_of(k)
        return shifted(gram[at : at + 1, :], first) if first else gram[at : at + 1, :]

    by_re = total_of(of_power(k) * v.re[0:1] for k, v in update.items()) * scale
    by_im = total_of(of_power(k) * v.im[0:1] for k, v in update.items()) * scale
    first_re = lanes(jnp.where(same, by_re - shifted(by_im, count), 0.0))
    first_im = lanes(jnp.where(same, by_im + shifted(by_re, count), 0.0))

    table = jnp.where(lane < count, table, 0.0) * (0.5 * scale)

    def across(col):
        return sublanes(jnp.where(same, col, 0.0))

    def mixed(col_re, col_im):
        def halves(col):
            straight = lanes(table * across(col))
            turned = lanes(jnp.where(same, sublanes(table * col), 0.0))
            return straight + turned, straight - turned

        re_re, im_re = halves(col_re)
        re_im, im_im = halves(col_im)
        return re_re - im_im, re_im + im_re

    mixed_re, mixed_im = mixed(first_re, first_im)
    second_re, second_im = first_re - mixed_re, first_im - mixed_im
    again_re, again_im = mixed(second_re, second_im)
    change = (
        -2.0 * (first_re * first_re + first_im * first_im)
        + (first_re * mixed_re + first_im * mixed_im)
        - 2.0 * (second_re * second_re + second_im * second_im)
        + (second_re * again_re + second_im * again_im)
    )
    final_sq = update_sq[0:1, 0:1] + sublanes(change)
    inverse = 1.0 / jnp.sqrt(final_sq + EPSILON)
    column[0] = jnp.broadcast_to((first_re + second_re) * inverse, (count, 128))
    column[1] = jnp.broadcast_to((first_im + second_im) * inverse, (count, 128))
    full_inverse = jnp.broadcast_to(inverse, tile)
    coefs = {k: v * full_inverse for k, v in update.items()}

    def wide(x):
        return jnp.tile(x[0:1, :], (1, width // 128))

    coefs = {k: Cx(wide(v.re), wide(v.im)) for k, v in coefs.items()}
    for a in range(rows):
        span = slice(a * depth, (a + 1) * depth)
        real = jnp.zeros((depth, width), jnp.float32)
        imag = real
        for k, v in coefs.items():
            re, im = powers[k][0, span, :], powers[k][1, span, :]
            real = real + (v.re * re - v.im * im)
            imag = imag + (v.re * im + v.im * re)
        for i in range(count):
            v = Cx(wide(column[0, i : i + 1, :]), wide(column[1, i : i + 1, :]))
            re, im = basis[i, 0, span, :], basis[i, 1, span, :]
            real = real - (v.re * re - v.im * im)
            imag = imag - (v.re * im + v.im * re)
        out[0, span, :] = real
        out[1, span, :] = imag


def on_device(
    search_basis, coefficients, target_shift, stiffness_diag, flame_mats,
    flame_count, flame_line, flame_burner, reference_part, reference_line,
):
    n_azim, n_dom = lax.axis_size("azim"), lax.axis_size("dom")
    count, _, rows, depth, width = search_basis.shape
    lines = rows * depth
    scale = 1.0 / float(stiffness_diag.size * n_azim * n_dom)
    slots = flame_mats.shape[0]
    base = 2 * rows
    tall = base + 2 * reference_part.shape[0]
    basis = search_basis.reshape(count, 2, lines, width)
    diag = stiffness_diag.reshape(lines, width)
    mats = flame_mats.reshape(slots, 2 * width, width)

    def exchange(values, axis, pairs):
        both = pairs + [(j, i) for i, j in pairs]
        return lax.ppermute(values, axis, both)

    azim_even = [(i, i + 1) for i in range(0, n_azim, 2)]
    azim_odd = [(i, (i + 1) % n_azim) for i in range(1, n_azim, 2)]
    dom_even = [(i, i + 1) for i in range(0, n_dom, 2)]
    dom_odd = [(i, (i + 1) % n_dom) for i in range(1, n_dom, 2)]

    def shape(*dims):
        return jax.ShapeDtypeStruct(dims, jnp.float32)

    fields = [
        shape(2, lines, width),
        shape(2, depth, width),
        shape(2, depth, width),
        shape(tall, width),
        shape(tall, width),
    ]
    (mats_in,) = held_in_hbm(mats)
    blocks = jax.ShapeDtypeStruct(mats.shape, mats.dtype)
    second, third = max(2, slots // 4), max(2, slots * 5 // 8)
    power, azim_x, azim_y, dom_x, dom_y, basis, mats = call(
        functools.partial(start_kernel, rows, depth),
        [*fields, shape(count, 2, lines, width), blocks],
        in_hbm(5),
        [*held_in_hbm(coefficients, reference_part, reference_line, basis), mats_in],
        [
            SMEM(coefficients.shape, jnp.float32),
            SMEM(reference_part.shape, jnp.int32),
            SMEM(reference_line.shape, jnp.int32),
            pltpu.SemaphoreType.DMA((3,)),
            pltpu.SemaphoreType.DMA((4,)),
            pltpu.SemaphoreType.DMA((second,)),
        ],
        cost=4,
    )
    powers = [power]
    held = VMEM((2 * count + 16, 128), jnp.float32)
    tiles = VMEM((width // 128, count * 2 * (lines // (INNER_STEPS + 1)), 128), jnp.float32)
    is_sum = lax.broadcasted_iota(jnp.int32, (tall, width), 0) >= base
    for step in range(INNER_STEPS + 1):
        from_dx = exchange(dom_x, "dom", dom_even)
        from_ax = exchange(azim_x, "azim", azim_even)
        from_ay = exchange(azim_y, "azim", azim_odd)
        dom_y = jnp.where(is_sum, dom_x + from_dx, dom_y)
        from_dy = exchange(dom_y, "dom", dom_odd)
        sums = dom_y + from_dy
        reach = 4
        while reach < n_dom:
            pairs = [(i, i ^ reach) for i in range(n_dom) if i < i ^ reach]
            sums = sums + exchange(sums, "dom", pairs)
            reach *= 2
        source = VMEM((16, width), jnp.bfloat16)
        if step == 0:
            dots, mats, live = call(
                functools.partial(first_dots_kernel, second),
                [shape(4, 128), blocks, jax.ShapeDtypeStruct((8, 128), jnp.int32)],
                vmem(4) + in_hbm(1),
                (basis, power, flame_count.reshape(1, 1), mats, mats_in),
                [held, tiles, pltpu.SemaphoreType.DMA((third - second,))],
                cost=2,
                aliases={3: 1},
            )
        else:
            given = (basis, *powers, dots)
            dots = call(
                functools.partial(dots_kernel, step),
                shape(4, 128),
                vmem(len(given)),
                given,
                [held, tiles],
            )
        numbers = (live, flame_line, flame_burner)
        if step == 0:
            flame, mats = call(
                functools.partial(first_flame_kernel, base, third),
                [shape(2, lines, width), blocks],
                smem(3) + vmem(2) + in_hbm(1) + vmem(1),
                (*numbers, sums, mats, mats_in, dots),
                [source, pltpu.SemaphoreType.DMA((slots - third,))],
                cost=3,
                aliases={4: 1},
            )
        else:
            flame = call(
                functools.partial(flame_kernel, base),
                shape(2, lines, width),
                smem(3) + vmem(3),
                (*numbers, sums, mats, dots),
                [source],
                cost=3,
            )
        received = (power, flame, diag, from_ax, from_ay, from_dx, from_dy)
        if step < INNER_STEPS:
            power, azim_x, azim_y, dom_x, dom_y = call(
                functools.partial(step_kernel, rows, depth),
                fields,
                smem(2) + vmem(7),
                (reference_part, reference_line, *received),
            )
        else:
            dots = call(
                functools.partial(last_kernel, rows, depth),
                shape(4, 128),
                vmem(8 + len(powers)),
                (*received, *powers, dots),
                [VMEM((2, lines, width), jnp.float32), held],
            )
        powers.append(power)
    devices = n_azim * n_dom
    spread = jnp.broadcast_to(dots[None], (devices, *dots.shape))
    gram = jnp.sum(lax.all_to_all(spread, ("azim", "dom"), 0, 0), axis=0)
    new_vector, ritz = call(
        functools.partial(end_kernel, rows, depth, scale),
        [shape(2, lines, width), shape(2)],
        smem(2) + vmem(2 + INNER_STEPS + 1),
        (target_shift, gram, gram, basis, *powers[: INNER_STEPS + 1]),
        [VMEM((2, count, 128), jnp.float32)],
        out_specs=[pl.BlockSpec(memory_space=VMEM), pl.BlockSpec(memory_space=SMEM)],
    )
    return new_vector.reshape(2, rows, depth, width), ritz


def solution(mesh):
    placed = (
        P(None, None, "azim", "dom", None),
        P(),
        P(),
        P("azim", "dom", None),
        P(("azim", "dom"), None, None, None),
        P(("azim", "dom")),
        P(("azim", "dom")),
        P(("azim", "dom")),
        P("azim"),
        P("azim"),
    )
    return jax.shard_map(
        on_device,
        mesh=mesh,
        in_specs=placed,
        out_specs=(P(None, "azim", "dom", None), P()),
        check_vma=False,
    )
```

```python
import functools

import jax
import jax.numpy as jnp
from jax import lax
from jax.experimental import pallas as pl
from jax.experimental.pallas import tpu as pltpu
from jax.sharding import PartitionSpec as P


INNER_STEPS = 3
EPSILON = 1e-06
CENTRE = 7.125
HIGHEST = lax.Precision.HIGHEST
VMEM = pltpu.VMEM
SMEM = pltpu.SMEM


def vmem(count):
    return [pl.BlockSpec(memory_space=VMEM) for _ in range(count)]


def smem(count):
    return [pl.BlockSpec(memory_space=SMEM) for _ in range(count)]


def in_hbm(count):
    return [pl.BlockSpec(memory_space=pltpu.HBM) for _ in range(count)]


def held_in_hbm(*arrays):
    return [pltpu.with_memory_space_constraint(a, pltpu.HBM) for a in arrays]


def call(kernel, outs, specs, args, scratch=(), cost=1, out_specs=None, aliases={}, limit=8 << 20):
    estimate = pl.CostEstimate(flops=0, transcendentals=0, bytes_accessed=cost * 2_000_000)
    if out_specs is None:
        out_specs = jax.tree.map(lambda _: pl.BlockSpec(memory_space=VMEM), outs)
    return pl.pallas_call(
        kernel,
        out_shape=outs,
        in_specs=specs,
        out_specs=out_specs,
        scratch_shapes=list(scratch),
        input_output_aliases=aliases,
        compiler_params=pltpu.CompilerParams(vmem_limit_bytes=limit),
        cost_estimate=estimate,
    )(*args)


def write_edges(rows, depth, field, ref_part, ref_line, azim_x, azim_y, dom_x, dom_y):
    odd_a = lax.axis_index("azim") % 2
    part = lax.axis_index("dom")
    odd_d = part % 2
    last = (rows - 1) * depth
    x_start = pl.multiple_of((1 - odd_a) * last, depth)
    y_start = pl.multiple_of(odd_a * last, depth)
    for c in range(2):
        azim_x[c] = field[c, pl.ds(x_start, depth), :]
        azim_y[c] = field[c, pl.ds(y_start, depth), :]
        for a in range(rows):
            x_row = a * depth + (1 - odd_d) * (depth - 1)
            y_row = a * depth + odd_d * (depth - 1)
            at = c * rows + a
            dom_x[at : at + 1, :] = field[c, pl.ds(x_row, 1), :]
            dom_y[at : at + 1, :] = field[c, pl.ds(y_row, 1), :]
    base = 2 * rows
    for b in range(ref_part.shape[0]):
        mine = ref_part[b] == part
        for c in range(2):
            at = base + 2 * b + c
            line = field[c, pl.ds(ref_line[b], 1), :]
            dom_x[at : at + 1, :] = jnp.where(mine, line, 0.0)
            dom_y[at : at + 1, :] = jnp.zeros_like(line)


def bring(source, target, first, sems):
    return [
        pltpu.make_async_copy(source.at[first + s], target.at[first + s], sems.at[s])
        for s in range(sems.shape[0])
    ]


def start_kernel(
    rows, depth, coef_in, part_in, line_in, basis_in, mats_in,
    field, azim_x, azim_y, dom_x, dom_y, basis, mats,
    coef, ref_part, ref_line, small_sems, sems, block_sems,
):
    count = basis.shape[0]
    pairs = ((coef_in, coef), (part_in, ref_part), (line_in, ref_line))
    small = [pltpu.make_async_copy(a, b, small_sems.at[i]) for i, (a, b) in enumerate(pairs)]
    group = count // sems.shape[0]
    large = [
        pltpu.make_async_copy(
            basis_in.at[pl.ds(i * group, group)], basis.at[pl.ds(i * group, group)], sems.at[i]
        )
        for i in range(sems.shape[0])
    ]
    blocks = bring(mats_in, mats, 0, block_sems)
    for copy in small + large + blocks:
        copy.start()
    for copy in small:
        copy.wait()
    for at, copy in enumerate(large):
        copy.wait()
        for a in range(rows):
            span = slice(a * depth, (a + 1) * depth)
            real = imag = None
            for i in range(at * group, (at + 1) * group):
                re, im = basis[i, 0, span, :], basis[i, 1, span, :]
                one = coef[0, i] * re - coef[1, i] * im
                two = coef[0, i] * im + coef[1, i] * re
                real = one if real is None else real + one
                imag = two if imag is None else imag + two
            field[0, span, :] = real if at == 0 else field[0, span, :] + real
            field[1, span, :] = imag if at == 0 else field[1, span, :] + imag
    write_edges(rows, depth, field, ref_part, ref_line, azim_x, azim_y, dom_x, dom_y)
    for copy in blocks:
        copy.wait()


def basis_products(part, parts, basis, tiles):
    half = basis.shape[0]
    count = 2 * half
    lines, width = basis.shape[2] // parts, basis.shape[3]
    first = part * lines
    for c in range(2):
        for i in range(half):
            for j in range(width // 128):
                at = (c * half + i) * lines
                tiles[j, at : at + lines, :] = basis[
                    i, c, first : first + lines, j * 128 : (j + 1) * 128
                ]

    def one(line):
        tall = jnp.concatenate(
            [tiles.at[j][pl.ds(line, count, stride=lines), :] for j in range(width // 128)], axis=1
        )
        high = tall.astype(jnp.bfloat16)
        low = (tall - high.astype(jnp.float32)).astype(jnp.bfloat16)
        return jnp.concatenate([high, low], axis=0)

    group = min(4, lines)

    def some(at, total):
        both = jnp.concatenate([one(at * group + i) for i in range(group)], axis=1)
        return total + lax.dot_general(
            both, both, (((1,), (1,)), ((), ())), preferred_element_type=jnp.float32
        )

    zero = jnp.zeros((2 * count, 2 * count), jnp.float32)
    total = lax.fori_loop(0, lines // group, some, zero)
    total = total[:count] + total[count:]
    total = jnp.concatenate([total, jnp.zeros((count, 128 - 2 * count), jnp.float32)], axis=1)
    total = total + pltpu.roll(total, 128 - count, 1)
    top, bottom = total[:half], total[half:]
    crossed = pltpu.roll(top, 128 - half, 1)
    lane = lax.broadcasted_iota(jnp.int32, (half, 128), 1)
    table = jnp.where(
        lane < half, top + pltpu.roll(bottom, 128 - half, 1) + crossed - bottom, 0.0
    )
    folds = 128 // half
    packed = []
    for r in range(half // folds):
        rows = [
            pltpu.roll(table[r * folds + s : r * folds + s + 1], half * s, 1) if s
            else table[r * folds : r * folds + 1]
            for s in range(folds)
        ]
        packed.append(total_of(rows))
    return packed


def add_basis_products(part, basis, tiles, dots):
    for r, row in enumerate(basis_products(part, INNER_STEPS + 1, basis, tiles)):
        dots[2 + r : 3 + r, :] += row


def dots_kernel(k, basis, *refs):
    powers, (dots_out, held, tiles) = refs[: k + 1], refs[-3:]
    add_dots(k, basis, powers[:-1], powers[-1], refs[k + 1], dots_out, held)
    add_basis_products(k, basis, tiles, dots_out)


def first_dots_kernel(
    first, basis, power, count, given, mats_in, dots_out, mats, count_out, held, tiles, sems
):
    copies = bring(mats_in, mats, first, sems)
    for copy in copies:
        copy.start()
    add_dots(0, basis, [], power, None, dots_out, held)
    add_basis_products(0, basis, tiles, dots_out)
    count_out[...] = jnp.broadcast_to(count[...], count_out.shape)
    for copy in copies:
        copy.wait()


def flame_kernel(base, live, lines, burners, sums, mats, *refs, ready=None):
    out, source = refs[-2:]
    width = sums.shape[1]
    slots = mats.shape[0]
    rows = sums.shape[0] - base
    source[...] = jnp.zeros_like(source)
    for i in range(rows):
        row = sums[base + i : base + i + 1, :]
        high = row.astype(jnp.bfloat16)
        source[2 * i : 2 * i + 1, :] = high
        source[2 * i + 1 : 2 * i + 2, :] = (row - high.astype(jnp.float32)).astype(jnp.bfloat16)
    out[...] = jnp.zeros_like(out)
    left = source[...]

    def products(blocks):
        return lax.dot_general(
            left, blocks, (((1,), (1,)), ((), ())), preferred_element_type=jnp.float32
        )

    def put(s, product):
        chosen = product[0:4]
        for b in range(1, rows // 2):
            chosen = jnp.where(burners[s] == b, product[4 * b : 4 * b + 4], chosen)
        by_re = chosen[0:1] + chosen[1:2]
        by_im = chosen[2:3] + chosen[3:4]
        at = pl.ds(lines[s], 1)
        out[0, at, :] += by_re[:, :width] - by_im[:, width:]
        out[1, at, :] += by_im[:, :width] + by_re[:, width:]

    def put_all(first, number):
        blocks = mats[first : first + number]
        every = products(blocks.reshape(number * 2 * width, width))
        for s in range(number):

            @pl.when(first + s < live[0, 0])
            def _():
                put(first + s, every[:, 2 * width * s : 2 * width * (s + 1)])

    few = 2

    @pl.when(live[0, 0] <= few)
    def _():
        def slot(s, carry):
            put(s, products(mats[s]))
            return carry

        lax.fori_loop(0, live[0, 0], slot, 0)

    if ready is None:

        @pl.when(live[0, 0] > few)
        def _():
            put_all(0, slots)
    else:
        there, wait = ready

        @pl.when(live[0, 0] > few)
        def _():
            put_all(0, there)

        wait()

        @pl.when(live[0, 0] > there)
        def _():
            put_all(there, slots - there)


def first_flame_kernel(
    base, first, live, lines, burners, sums, given, mats_in, order, out, mats, source, sems
):
    copies = bring(mats_in, mats, first, sems)
    for copy in copies:
        copy.start()

    def ready():
        for copy in copies:
            copy.wait()

    flame_kernel(base, live, lines, burners, sums, mats, order, out, source, ready=(first, ready))


def step_kernel(
    rows, depth, ref_part, ref_line, old, flame, diag, from_ax, from_ay, from_dx, from_dy,
    field, azim_x, azim_y, dom_x, dom_y,
):
    width = old.shape[2]
    odd_a = lax.axis_index("azim") % 2 == 1
    part = lax.axis_index("dom")
    odd_d = part % 2 == 1
    row_at = lax.broadcasted_iota(jnp.int32, (depth, width), 0)
    lane_at = lax.broadcasted_iota(jnp.int32, (depth, width), 1)
    for c in range(2):
        before = jnp.where(odd_a, from_ax[c], from_ay[c])
        after = jnp.where(odd_a, from_ay[c], from_ax[c])
        planes = [old[c, a * depth : (a + 1) * depth, :] for a in range(rows)]
        around = [before, *planes, after]
        for a in range(rows):
            here = planes[a]
            at = c * rows + a
            one, two = from_dx[at : at + 1, :], from_dy[at : at + 1, :]
            inner = jnp.where(part == 0, 0.0, jnp.where(odd_d, one, two))
            outer = jnp.where(part == lax.axis_size("dom") - 1, 0.0, jnp.where(odd_d, two, one))
            down = jnp.where(row_at == 0, inner, pltpu.roll(here, 1, 0))
            up = jnp.where(row_at == depth - 1, outer, pltpu.roll(here, depth - 1, 0))
            left = jnp.where(lane_at == 0, 0.0, pltpu.roll(here, 1, 1))
            right = jnp.where(lane_at == width - 1, 0.0, pltpu.roll(here, width - 1, 1))
            beside = (around[a] + around[a + 2]) + (down + up) + (left + right)
            span = slice(a * depth, (a + 1) * depth)
            factor = diag[span, :] + (6.0 - CENTRE)
            field[c, span, :] = factor * here - beside + flame[c, span, :]
    if azim_x is not None:
        write_edges(rows, depth, field, ref_part, ref_line, azim_x, azim_y, dom_x, dom_y)


def last_kernel(rows, depth, *refs):
    first, powers, (dots_in, dots_out, field, held) = refs[:7], refs[7:-4], refs[-4:]
    step_kernel(rows, depth, None, None, *first, field, None, None, None, None)
    add_dots(len(powers), None, powers, field, dots_in, dots_out, held)


def folded(x):
    tall = total_of(x[i : i + 8] for i in range(0, x.shape[0], 8))
    tile = total_of(tall[:, j : j + 128] for j in range(0, x.shape[1], 128))
    return jnp.sum(tile, axis=0, keepdims=True)


def total_of(terms):
    terms = list(terms)
    while len(terms) > 1:
        terms = [
            terms[i] + terms[i + 1] if i + 1 < len(terms) else terms[i]
            for i in range(0, len(terms), 2)
        ]
    return terms[0]


def place_of(k):
    return (0, 16) if k == INNER_STEPS + 1 else (k // 2, 64 * (k % 2))


def add_dots(k, basis, powers, current, dots_in, dots_out, held):
    held[...] = jnp.zeros_like(held)
    re, im = current[0], current[1]
    count = 0
    if basis is not None:
        count = basis.shape[0]

        def one(i, carry):
            left_re, left_im = basis[i, 0], basis[i, 1]
            held[pl.ds(i, 1), :] = folded(left_re * re + left_im * im)
            held[pl.ds(count + i, 1), :] = folded(left_re * im - left_im * re)
            return carry

        lax.fori_loop(0, count, one, 0, unroll=4)
    first = held.shape[0] - 16
    for j, power in enumerate([*powers, current]):
        left_re, left_im = power[0], power[1]
        held[first + j : first + j + 1, :] = folded(left_re * re + left_im * im)
        held[first + 8 + j : first + 9 + j, :] = folded(left_re * im - left_im * re)
    row = lax.dot_general(
        jnp.ones((8, 128), jnp.float32), held[...], (((1,), (1,)), ((), ())),
        precision=HIGHEST, preferred_element_type=jnp.float32,
    )
    row = jnp.concatenate([row, jnp.zeros((8, 128 - row.shape[1]), jnp.float32)], axis=1)
    at, lane = place_of(k)
    row = pltpu.roll(row, lane, 1) if lane else row
    dots_out[...] = jnp.zeros_like(dots_out) if dots_in is None else dots_in[...]
    dots_out[at : at + 1, :] += row[0:1]


class Cx:
    def __init__(self, re, im):
        self.re, self.im = re, im

    def __add__(self, o):
        return Cx(self.re + o.re, self.im + o.im)

    def __sub__(self, o):
        return Cx(self.re - o.re, self.im - o.im)

    def __mul__(self, o):
        if isinstance(o, Cx):
            return Cx(self.re * o.re - self.im * o.im, self.re * o.im + self.im * o.re)
        return Cx(self.re * o, self.im * o)

    def conj(self):
        return Cx(self.re, -self.im)

    def sq(self):
        return self.re * self.re + self.im * self.im


def small_problem(gram, mu):
    steps = INNER_STEPS

    def applied(vec):
        return {j: total_of(gram[j][k] * v for k, v in vec.items()) for j in range(steps + 2)}

    def dot(left, image):
        return total_of(v.conj() * image[k] for k, v in left.items())

    def less(vec, scale, other):
        out = dict(vec)
        for k, v in other.items():
            out[k] = out[k] - scale * v if k in out else Cx(-(scale * v).re, -(scale * v).im)
        return out

    def scaled(vec, by):
        return {k: v * by for k, v in vec.items()}

    def times_operator(vec, shift):
        out = {}
        for k, v in vec.items():
            out[k + 1] = v
        for k, v in vec.items():
            out[k] = out[k] + shift * v if k in out else shift * v
        return out

    first = gram[0][0].re
    unit = 1.0 / jnp.sqrt(first + EPSILON)
    zero = jnp.zeros_like(first)
    u = {0: Cx(unit, zero)}
    u_image = applied(u)
    w = times_operator(u, mu)
    w_image = applied(w)
    image_sq = dot(w, w_image).re
    cross = dot(w, u_image)
    bottom = cross.sq()
    theta = Cx(image_sq * cross.re / bottom, -image_sq * cross.im / bottom)
    r = less(w, theta, u)
    along = dot(u, applied(r))
    b = scaled(less(r, along, u), -1.0)
    beta = jnp.sqrt(dot(b, applied(b)).re + EPSILON)
    q = [scaled(b, 1.0 / beta)]
    q_image = [applied(q[0])]
    hess = []
    shift = mu - theta
    for column in range(steps):
        z = times_operator(q[-1], shift)
        z = less(z, dot(u, applied(z)), u)
        z_image = applied(z)
        column_dots = [dot(one, z_image) for one in q]
        for value, one in zip(column_dots, q):
            z = less(z, value, one)
        z_image = applied(z)
        length = jnp.sqrt(dot(z, z_image).re + EPSILON)
        hess.append((column_dots, length))
        if column + 1 < steps:
            q.append(scaled(z, 1.0 / length))
    full = []
    for column, (dots, length) in enumerate(hess):
        entries = {i: v for i, v in enumerate(dots)}
        entries[column + 1] = Cx(length, zero)
        full.append(entries)

    def column_dot(i, j):
        return total_of(full[i][k].conj() * full[j][k] for k in full[i] if k in full[j])

    low = [[None] * steps for _ in range(steps)]
    for j in range(steps):
        diagonal = column_dot(j, j).re
        for k in range(j):
            diagonal = diagonal - low[j][k].sq()
        root = jnp.sqrt(diagonal)
        low[j][j] = root
        for i in range(j + 1, steps):
            value = column_dot(i, j)
            for k in range(j):
                value = value - low[i][k] * low[j][k].conj()
            low[i][j] = value * (1.0 / root)
    middle = []
    for i in range(steps):
        value = full[i][0].conj() * beta
        for k in range(i):
            value = value - low[i][k] * middle[k]
        middle.append(value * (1.0 / low[i][i]))
    solved = [None] * steps
    for i in reversed(range(steps)):
        value = middle[i]
        for k in range(i + 1, steps):
            value = value - low[k][i].conj() * solved[k]
        solved[i] = value * (1.0 / low[i][i])
    update = {}
    for value, one in zip(solved, q):
        for k, v in one.items():
            update[k] = update[k] + value * v if k in update else value * v
    update_sq = dot(update, applied(update)).re
    return theta, update, update_sq


def end_kernel(rows, depth, scale, shift, gram_s, gram, basis, *refs):
    powers, out, ritz, column = refs[: INNER_STEPS + 1], refs[-3], refs[-2], refs[-1]
    count = basis.shape[0]
    width = basis.shape[3]
    base = 2 * count
    tile = (8, 128)

    def splat(i, j):
        return jnp.full(tile, gram_s[i, j] * scale, jnp.float32)

    size = INNER_STEPS + 2
    table = [[None] * size for _ in range(size)]
    for i in range(size):
        for j in range(i, size):
            at, first = place_of(j)
            first += base + i
            im = splat(at, first + 8) if i != j else jnp.zeros(tile, jnp.float32)
            table[i][j] = Cx(splat(at, first), im)
            if i != j:
                table[j][i] = table[i][j].conj()
    mu = Cx(
        jnp.full(tile, CENTRE - shift[0], jnp.float32), jnp.full(tile, -shift[1], jnp.float32)
    )
    theta, update, update_sq = small_problem(table, mu)
    ritz[0] = theta.re[0, 0]
    ritz[1] = theta.im[0, 0]

    def lanes(x):
        return jnp.sum(x, axis=1, keepdims=True)

    def sublanes(x):
        return jnp.sum(x, axis=0, keepdims=True)

    def shifted(x, by):
        return pltpu.roll(x, 128 - by, 1)

    folds = 128 // count
    table = jnp.concatenate(
        [
            shifted(gram[2 + r : 3 + r, :], count * q) if q else gram[2 + r : 3 + r, :]
            for r in range(count // folds)
            for q in range(folds)
        ],
        axis=0,
    )
    lane = lax.broadcasted_iota(jnp.int32, (count, 128), 1)
    same = lax.broadcasted_iota(jnp.int32, (count, 128), 0) == lane

    def of_power(k):
        at, first = place_of(k)
        return shifted(gram[at : at + 1, :], first) if first else gram[at : at + 1, :]

    by_re = total_of(of_power(k) * v.re[0:1] for k, v in update.items()) * scale
    by_im = total_of(of_power(k) * v.im[0:1] for k, v in update.items()) * scale
    first_re = lanes(jnp.where(same, by_re - shifted(by_im, count), 0.0))
    first_im = lanes(jnp.where(same, by_im + shifted(by_re, count), 0.0))

    table = jnp.where(lane < count, table, 0.0) * (0.5 * scale)

    def across(col):
        return sublanes(jnp.where(same, col, 0.0))

    def mixed(col_re, col_im):
        def halves(col):
            straight = lanes(table * across(col))
            turned = lanes(jnp.where(same, sublanes(table * col), 0.0))
            return straight + turned, straight - turned

        re_re, im_re = halves(col_re)
        re_im, im_im = halves(col_im)
        return re_re - im_im, re_im + im_re

    mixed_re, mixed_im = mixed(first_re, first_im)
    second_re, second_im = first_re - mixed_re, first_im - mixed_im
    again_re, again_im = mixed(second_re, second_im)
    change = (
        -2.0 * (first_re * first_re + first_im * first_im)
        + (first_re * mixed_re + first_im * mixed_im)
        - 2.0 * (second_re * second_re + second_im * second_im)
        + (second_re * again_re + second_im * again_im)
    )
    final_sq = update_sq[0:1, 0:1] + sublanes(change)
    inverse = 1.0 / jnp.sqrt(final_sq + EPSILON)
    column[0] = jnp.broadcast_to((first_re + second_re) * inverse, (count, 128))
    column[1] = jnp.broadcast_to((first_im + second_im) * inverse, (count, 128))
    full_inverse = jnp.broadcast_to(inverse, tile)
    coefs = {k: v * full_inverse for k, v in update.items()}

    def wide(x):
        return jnp.tile(x[0:1, :], (1, width // 128))

    coefs = {k: Cx(wide(v.re), wide(v.im)) for k, v in coefs.items()}
    for start in range(0, rows * depth, 8):
        span = slice(start, start + 8)
        real = imag = None
        for k, v in coefs.items():
            re, im = powers[k][0, span, :], powers[k][1, span, :]
            one, two = v.re * re - v.im * im, v.re * im + v.im * re
            real = one if real is None else real + one
            imag = two if imag is None else imag + two
        for i in range(count):
            v = Cx(wide(column[0, i : i + 1, :]), wide(column[1, i : i + 1, :]))
            re, im = basis[i, 0, span, :], basis[i, 1, span, :]
            real = real - (v.re * re - v.im * im)
            imag = imag - (v.re * im + v.im * re)
        out[0, span, :] = real
        out[1, span, :] = imag


def on_device(
    search_basis, coefficients, target_shift, stiffness_diag, flame_mats,
    flame_count, flame_line, flame_burner, reference_part, reference_line,
):
    n_azim, n_dom = lax.axis_size("azim"), lax.axis_size("dom")
    count, _, rows, depth, width = search_basis.shape
    lines = rows * depth
    scale = 1.0 / float(stiffness_diag.size * n_azim * n_dom)
    slots = flame_mats.shape[0]
    base = 2 * rows
    tall = base + 2 * reference_part.shape[0]
    basis = search_basis.reshape(count, 2, lines, width)
    diag = stiffness_diag.reshape(lines, width)
    mats = flame_mats.reshape(slots, 2 * width, width)

    def exchange(values, axis, pairs):
        both = pairs + [(j, i) for i, j in pairs]
        return lax.ppermute(values, axis, both)

    azim_even = [(i, i + 1) for i in range(0, n_azim, 2)]
    azim_odd = [(i, (i + 1) % n_azim) for i in range(1, n_azim, 2)]
    dom_even = [(i, i + 1) for i in range(0, n_dom, 2)]
    dom_odd = [(i, (i + 1) % n_dom) for i in range(1, n_dom, 2)]

    def shape(*dims):
        return jax.ShapeDtypeStruct(dims, jnp.float32)

    fields = [
        shape(2, lines, width),
        shape(2, depth, width),
        shape(2, depth, width),
        shape(tall, width),
        shape(tall, width),
    ]
    (mats_in,) = held_in_hbm(mats)
    blocks = jax.ShapeDtypeStruct(mats.shape, mats.dtype)
    second, third = max(2, slots // 4), max(2, slots * 5 // 8)
    power, azim_x, azim_y, dom_x, dom_y, basis, mats = call(
        functools.partial(start_kernel, rows, depth),
        [*fields, shape(count, 2, lines, width), blocks],
        in_hbm(5),
        [*held_in_hbm(coefficients, reference_part, reference_line, basis), mats_in],
        [
            SMEM(coefficients.shape, jnp.float32),
            SMEM(reference_part.shape, jnp.int32),
            SMEM(reference_line.shape, jnp.int32),
            pltpu.SemaphoreType.DMA((3,)),
            pltpu.SemaphoreType.DMA((4,)),
            pltpu.SemaphoreType.DMA((second,)),
        ],
        cost=4,
    )
    powers = [power]
    held = VMEM((2 * count + 16, 128), jnp.float32)
    tiles = VMEM((width // 128, count * 2 * (lines // (INNER_STEPS + 1)), 128), jnp.float32)
    is_sum = lax.broadcasted_iota(jnp.int32, (tall, width), 0) >= base
    for step in range(INNER_STEPS + 1):
        from_dx = exchange(dom_x, "dom", dom_even)
        from_ax = exchange(azim_x, "azim", azim_even)
        from_ay = exchange(azim_y, "azim", azim_odd)
        dom_y = jnp.where(is_sum, dom_x + from_dx, dom_y)
        from_dy = exchange(dom_y, "dom", dom_odd)
        sums = dom_y + from_dy
        reach = 4
        while reach < n_dom:
            pairs = [(i, i ^ reach) for i in range(n_dom) if i < i ^ reach]
            sums = sums + exchange(sums, "dom", pairs)
            reach *= 2
        source = VMEM((16, width), jnp.bfloat16)
        if step == 0:
            dots, mats, live = call(
                functools.partial(first_dots_kernel, second),
                [shape(4, 128), blocks, jax.ShapeDtypeStruct((8, 128), jnp.int32)],
                vmem(4) + in_hbm(1),
                (basis, power, flame_count.reshape(1, 1), mats, mats_in),
                [held, tiles, pltpu.SemaphoreType.DMA((third - second,))],
                cost=2,
                aliases={3: 1},
            )
        else:
            given = (basis, *powers, dots)
            dots = call(
                functools.partial(dots_kernel, step),
                shape(4, 128),
                vmem(len(given)),
                given,
                [held, tiles],
            )
        numbers = (live, flame_line, flame_burner)
        if step == 0:
            flame, mats = call(
                functools.partial(first_flame_kernel, base, third),
                [shape(2, lines, width), blocks],
                smem(3) + vmem(2) + in_hbm(1) + vmem(1),
                (*numbers, sums, mats, mats_in, dots),
                [source, pltpu.SemaphoreType.DMA((slots - third,))],
                cost=3,
                aliases={4: 1},
            )
        else:
            flame = call(
                functools.partial(flame_kernel, base),
                shape(2, lines, width),
                smem(3) + vmem(3),
                (*numbers, sums, mats, dots),
                [source],
                cost=3,
            )
        received = (power, flame, diag, from_ax, from_ay, from_dx, from_dy)
        if step < INNER_STEPS:
            power, azim_x, azim_y, dom_x, dom_y = call(
                functools.partial(step_kernel, rows, depth),
                fields,
                smem(2) + vmem(7),
                (reference_part, reference_line, *received),
            )
        else:
            dots = call(
                functools.partial(last_kernel, rows, depth),
                shape(4, 128),
                vmem(8 + len(powers)),
                (*received, *powers, dots),
                [VMEM((2, lines, width), jnp.float32), held],
            )
        powers.append(power)
    devices = n_azim * n_dom
    spread = jnp.broadcast_to(dots[None], (devices, *dots.shape))
    gram = jnp.sum(lax.all_to_all(spread, ("azim", "dom"), 0, 0), axis=0)
    new_vector, ritz = call(
        functools.partial(end_kernel, rows, depth, scale),
        [shape(2, lines, width), shape(2)],
        smem(2) + vmem(2 + INNER_STEPS + 1),
        (target_shift, gram, gram, basis, *powers[: INNER_STEPS + 1]),
        [VMEM((2, count, 128), jnp.float32)],
        out_specs=[pl.BlockSpec(memory_space=VMEM), pl.BlockSpec(memory_space=SMEM)],
    )
    return new_vector.reshape(2, rows, depth, width), ritz


def solution(mesh):
    placed = (
        P(None, None, "azim", "dom", None),
        P(),
        P(),
        P("azim", "dom", None),
        P(("azim", "dom"), None, None, None),
        P(("azim", "dom")),
        P(("azim", "dom")),
        P(("azim", "dom")),
        P("azim"),
        P("azim"),
    )
    return jax.shard_map(
        on_device,
        mesh=mesh,
        in_specs=placed,
        out_specs=(P(None, "azim", "dom", None), P()),
        check_vma=False,
    )
```
